256 devices in a mesh: gx: 32 (over z, x), gy: 8 (over y, core).
Axes of the slice: x: 4, y: 4, z: 8, core: 2. Of those that a mesh axis runs over, the one named last changes fastest.
Arguments:
- krylov_block: float32 [16, 26, 256, 2048], P(None, None, 'gx', 'gy'), may hold values from -13 to 13
- prior_basis: float32 [24, 26, 256, 2048], P(None, None, 'gx', 'gy'), may hold values from -5.2 to 5.2
- flux_along: float32 [26, 26], replicated, may hold values from -1.25 to 1.25
- flux_across: float32 [26, 26], replicated, may hold values from -1.25 to 1.25
- collision: float32 [256, 2048], P('gx', 'gy'), may hold values from 1 to 10
- field_rates: float32 [26], replicated, may hold values from 0.5 to 2
- wall_table: float32 [4, 26], replicated, may hold values from 0.5 to 3
- wall_mask: int32 [256, 2048], P('gx', 'gy'), may hold values 0 or 1
- wall_type: int32 [256, 2048], P('gx', 'gy'), may hold values from 0 to 3
Outputs:
- new_block: float32 [16, 26, 256, 2048], P(None, None, 'gx', 'gy')
- projection: float32 [24, 16], replicated
- triangle: float32 [16, 16], replicated
The draws below stay inside these ranges and needn't reach their ends.
All inputs are finite; a program needn't handle non-finite values. No bound on the sum of `wall_mask` on one device may be relied on, other than what follows from the above.
Results may differ from the reference program's by a relative error of at most 0.0003.
Values sent between devices are 32-bit elements; how exact they have to be, the bound alone decides.
No kernel may reach another device: no remote copies, remote signals or barrier semaphores. Data moves between devices by JAX's collectives and lax.ppermute only.
A program may use at most 128 MiB of HBM per device.

```python
import math
import jax
import jax.numpy as jnp
from jax import lax

FIELDS = 26
BLOCK = 16
PRIOR = 24
TYPES = 4
NX = 256
NY = 2048


def rough_field(key, extent):
    return jax.random.truncated_normal(key, -4.0, 4.0, extent, jnp.float32)


def common_parts(key):
    folded = jax.random.fold_in(key, 7101)
    common = rough_field(jax.random.fold_in(folded, 1), (FIELDS, NX, NY))
    detail = rough_field(jax.random.fold_in(folded, 3), (BLOCK, FIELDS, NX, NY))
    return (common, detail)


def stratified(key, number, lowest):
    ranking = jax.random.permutation(jax.random.fold_in(key, 1), number).astype(jnp.float32)
    jitter = jax.random.uniform(jax.random.fold_in(key, 2), (number,), jnp.float32)
    return lowest * jnp.power(10.0, (ranking + jitter) / number)


def draw_krylov_block(key, part):
    common, detail = common_parts(key)
    column_scale = stratified(jax.random.fold_in(key, 7201), BLOCK, 0.3)
    mixing = stratified(jax.random.fold_in(key, 7202), BLOCK, 0.008)
    return column_scale[:, None, None, None] * (common[None] + mixing[:, None, None, None] * detail)


def draw_prior_basis(key, part):
    common, detail = common_parts(key)
    own_part = rough_field(jax.random.fold_in(key, 7301), (PRIOR, FIELDS, NX, NY))
    tilt_weight = jax.random.uniform(jax.random.fold_in(key, 7302), (PRIOR,), jnp.float32, -0.1, 0.1)
    linked = detail[jnp.arange(PRIOR) % BLOCK]
    scale_back = 1.0 / jnp.sqrt(1.0 + tilt_weight * tilt_weight + 0.04)
    mixed = own_part + tilt_weight[:, None, None, None] * common[None] + 0.2 * linked
    return scale_back[:, None, None, None] * mixed


def with_ends(values, key, smallest, high):
    longest = values.shape.index(max(values.shape))
    spots = []
    for shift in (0, 1):
        where = [jax.random.randint(jax.random.fold_in(key, axis), (), 0, length) for axis, length in enumerate(values.shape)]
        where[longest] = (where[longest] + shift) % values.shape[longest]
        spots.append(tuple(where))
    return values.at[spots[0]].set(smallest).at[spots[1]].set(high)


def level_of(rng, dims, pieces, least, top_value):
    loudness = 1.0
    for position, blocks in pieces:
        draws = jax.random.uniform(jax.random.fold_in(jax.random.fold_in(rng, 6), position), (blocks,), jnp.float32, least / len(pieces), top_value / len(pieces))
        loudness = loudness * jnp.repeat(jnp.exp(draws), dims[position] // blocks).reshape((-1,) + (1,) * (len(dims) - 1 - position))
    return loudness


def normal_values(key, dims, deviation, most, kind=jnp.bfloat16):
    return jnp.clip(deviation * jax.random.normal(key, dims, jnp.float32), -most, most).astype(kind)


def setup_inputs(seed: int = 0) -> dict:
    splits = jax.random.split(jax.random.key(seed), 10)
    return {
        "krylov_block": draw_krylov_block(jax.random.fold_in(splits[9], 71), 0),
        "prior_basis": draw_prior_basis(jax.random.fold_in(splits[9], 71), 0),
        "flux_along": normal_values(splits[2], (FIELDS, FIELDS), FIELDS ** -0.5, 1.25, jnp.float32),
        "flux_across": normal_values(splits[3], (FIELDS, FIELDS), FIELDS ** -0.5, 1.25, jnp.float32),
        "collision": jnp.clip(jnp.exp(math.log(10.0) - 2.3025851 * jax.random.uniform(splits[4], (NX, NY), jnp.float32) ** level_of(splits[4], (NX, NY), ((0, 32), (1, 8)), -0.2, 0.2)), 1.0, 10.0),
        "field_rates": jnp.clip(jnp.exp(jax.random.uniform(splits[5], (FIELDS,), jnp.float32, math.log(0.5), math.log(2.0))), 0.5, 2.0),
        "wall_table": jnp.clip(jax.random.uniform(splits[6], (TYPES, FIELDS), jnp.float32, 0.5, 3.0), 0.5, 3.0),
        "wall_mask": with_ends((jax.random.randint(splits[7], (NX, NY), 0, 4) < 1).astype(jnp.int32), jax.random.fold_in(splits[7], 1), 0, 1),
        "wall_type": with_ends(jax.random.randint(splits[8], (NX, NY), 0, TYPES), jax.random.fold_in(splits[8], 1), 0, TYPES - 1).astype(jnp.int32),
    }


damping = 0.0625
precise = lax.Precision.HIGHEST

def wall_gains(wall_mask, wall_type, wall_table):
    type_ids = jnp.arange(wall_table.shape[0], dtype=jnp.int32)
    onehot = (wall_type[None, :, :] == type_ids[:, None, None]).astype(jnp.float32)
    gains = jnp.einsum('txy,tf->fxy', onehot, wall_table, precision=precise)
    return gains * wall_mask.astype(jnp.float32)[None, :, :]

def operate_block(padded, local_coeff, flux_along, flux_across):
    rows_x = padded.shape[2] - 4
    rows_y = padded.shape[3] - 4

    def shifted(step_x, step_y):
        return padded[:, :, 2 + step_x:2 + step_x + rows_x, 2 + step_y:2 + step_y + rows_y]
    centre = shifted(0, 0)
    grad_x = 0.5 * (shifted(1, 0) - shifted(-1, 0))
    grad_y = 0.5 * (shifted(0, 1) - shifted(0, -1))
    fourth = shifted(-2, 0) - 4.0 * shifted(-1, 0) + 6.0 * centre - 4.0 * shifted(1, 0) + shifted(2, 0)
    fourth = fourth + shifted(0, -2) - 4.0 * shifted(0, -1) + 6.0 * centre - 4.0 * shifted(0, 1) + shifted(0, 2)
    result = local_coeff[None] * centre + damping * fourth
    result = result + jnp.einsum('fg,mgxy->mfxy', flux_along, grad_x, precision=precise)
    result = result + jnp.einsum('fg,mgxy->mfxy', flux_across, grad_y, precision=precise)
    return result

def inner_all(left, right):
    return jnp.einsum('kfxy,mfxy->km', left, right, precision=precise)

def mix_basis(weights, basis):
    return jnp.einsum('km,kfxy->mfxy', weights, basis, precision=precise)

def reference(krylov_block, prior_basis, flux_along, flux_across, collision, field_rates, wall_table, wall_mask, wall_type):
    inv_cells = 1.0 / (FIELDS * NX * NY)
    local_coeff = collision[None, :, :] * field_rates[:, None, None] + wall_gains(wall_mask, wall_type, wall_table)

    def apply_one(vector):
        padded = jnp.pad(vector[None], ((0, 0), (0, 0), (2, 2), (2, 2)))
        return operate_block(padded, local_coeff, flux_along, flux_across)[0]
    applied = lax.map(apply_one, krylov_block)
    first_pass = inner_all(prior_basis, applied) * inv_cells
    applied = applied - mix_basis(first_pass, prior_basis)
    second_pass = inner_all(prior_basis, applied) * inv_cells
    applied = applied - mix_basis(second_pass, prior_basis)
    projection = first_pass + second_pass
    identity_m = jnp.eye(BLOCK, dtype=jnp.float32)
    lower_one = jnp.linalg.cholesky(inner_all(applied, applied) * inv_cells)
    inv_one = jax.scipy.linalg.solve_triangular(lower_one, identity_m, lower=True)
    orthonormal = jnp.einsum('ij,jfxy->ifxy', inv_one, applied, precision=precise)
    lower_two = jnp.linalg.cholesky(inner_all(orthonormal, orthonormal) * inv_cells)
    inv_two = jax.scipy.linalg.solve_triangular(lower_two, identity_m, lower=True)
    new_block = jnp.einsum('ij,jfxy->ifxy', inv_two, orthonormal, precision=precise)
    triangle = jnp.dot(lower_one, lower_two, precision=precise).T
    return (new_block, projection, triangle)
```

```python
import functools

import jax
import jax.numpy as jnp
from jax import lax
from jax.experimental import pallas as pl
from jax.experimental.pallas import tpu as pltpu
from jax.sharding import Mesh
from jax.sharding import PartitionSpec as P

GX = ("gx_z", "gx_x")
GY = ("gy_y", "gy_c")
STAGES = (("gx_x", "gy_y"), ("gx_z", "gy_c"))

DAMP = 0.0625
PRECISE = lax.Precision.HIGHEST
F32 = jnp.float32
BF16 = jnp.bfloat16

M = 16
K = 24
F = 26
X = 8
Y = 256
FX = F * X
MX = M * X
KX = K * X
PAIRS = M // 2
HALO = 4 * F

NN = (((1,), (0,)), ((), ()))
NT = (((1,), (1,)), ((), ()))
TN = (((0,), (0,)), ((), ()))


def exact_dot(a, b, dims=NN):
    return lax.dot_general(a, b, dims, precision=PRECISE, preferred_element_type=F32)


def half_dot(a, b, dims=NN):
    return lax.dot_general(a, b, dims, preferred_element_type=F32)


def split2(v):
    hi = v.astype(BF16)
    return hi, (v - hi.astype(F32)).astype(BF16)


def split3(v):
    hi = v.astype(BF16)
    rest = v - hi.astype(F32)
    mid = rest.astype(BF16)
    return hi, mid, (rest - mid.astype(F32)).astype(BF16)


def iota(shape, dim):
    return lax.broadcasted_iota(jnp.int32, shape, dim)


def where0(mask, v):
    return jnp.where(mask, v, jnp.zeros_like(v))


def spread(small, rows, cols):
    n, k = small.shape
    left = (iota((rows, n), 0) // X == iota((rows, n), 1)).astype(F32)
    right = (iota((k, cols), 1) // X == iota((k, cols), 0)).astype(F32)
    return exact_dot(exact_dot(left, small), right)


def two_sum(a, b):
    s = a + b
    t = s - a
    return s, (a - (s - t)) + (b - t)


def roll(v, shift, axis):
    size = v.shape[axis]
    return pltpu.roll(v, shift % size if isinstance(shift, int) else shift, axis)


def pack_kernel(v_ref, first_ref, last_ref, yfirst_ref, ylast_ref, *, step_m):
    step = pl.program_id(0)
    for i in range(step_m):
        for f in range(F):
            at = (i % 2 * F + f) * 2
            first_ref[i // 2, at : at + 2, :] = v_ref[i, f, 0:2, :]
            last_ref[i // 2, at : at + 2, :] = v_ref[i, f, X - 2 : X, :]
    lane = iota((FX, 128), 1)
    at_first, at_last = yfirst_ref[...], ylast_ref[...]
    for i in range(step_m):
        m = step * step_m + i
        mine = lane // 2 == m
        left = v_ref[i, :, :, 0:128].reshape(FX, 128)
        right = v_ref[i, :, :, Y - 128 : Y].reshape(FX, 128)
        at_first = jnp.where(mine, roll(left, 2 * m, 1), at_first)
        at_last = jnp.where(mine, roll(right, 2 * m + 2, 1), at_last)
    keep = lane < 2 * step_m * (step + 1)
    yfirst_ref[...] = where0(keep, at_first)
    ylast_ref[...] = where0(keep, at_last)


def pack(v, step_m=4):
    return pl.pallas_call(
        functools.partial(pack_kernel, step_m=step_m),
        grid=(M // step_m,),
        in_specs=[pl.BlockSpec((step_m, F, X, Y), lambda i: (i, 0, 0, 0))],
        out_specs=[
            pl.BlockSpec((step_m // 2, HALO, Y), lambda i: (i, 0, 0)),
            pl.BlockSpec((step_m // 2, HALO, Y), lambda i: (i, 0, 0)),
            pl.BlockSpec((FX, 128), lambda i: (0, 0)),
            pl.BlockSpec((FX, 128), lambda i: (0, 0)),
        ],
        out_shape=[
            jax.ShapeDtypeStruct((PAIRS, HALO, Y), F32),
            jax.ShapeDtypeStruct((PAIRS, HALO, Y), F32),
            jax.ShapeDtypeStruct((FX, 128), F32),
            jax.ShapeDtypeStruct((FX, 128), F32),
        ],
        cost_estimate=pl.CostEstimate(flops=10**6, bytes_accessed=6 * 10**6, transcendentals=0),
        name="pack",
    )(v)


def inside_kernel(
    v_ref, along_ref, across_ref, coll_ref, mask_ref, type_ref, rate_ref, table_ref,
    out_ref, w_hi, w_lo, coeff, *, step_m,
):
    @pl.when(pl.program_id(0) == 0)
    def _():
        row, col = iota((FX, FX), 0), iota((FX, FX), 1)
        same_f = row // X == col // X
        step = col % X - row % X
        fa = spread(along_ref[...], FX, FX)
        fc = spread(across_ref[...], FX, FX)
        wx = where0(step == 1, 0.5 * fa) - where0(step == -1, 0.5 * fa)
        near = same_f & (jnp.abs(step) == 1)
        far = same_f & (jnp.abs(step) == 2)
        wx = wx + jnp.where(near, -4.0 * DAMP, 0.0) + jnp.where(far, DAMP, 0.0)
        wy = where0(step == 0, 0.5 * fc)
        hi, lo = split2(wx)
        w_hi[0:FX, :] = hi
        w_lo[0:FX, :] = lo
        hi, lo = split2(wy)
        w_hi[FX : 2 * FX, :] = hi
        w_lo[FX : 2 * FX, :] = lo
        walls = [
            jnp.where(type_ref[...] == t, mask_ref[...].astype(F32), 0.0)
            for t in range(table_ref.shape[0])
        ]
        for f in range(F):
            c = coll_ref[...] * rate_ref[f]
            for t, wall in enumerate(walls):
                c = c + wall * table_ref[t, f]
            coeff[f * X : (f + 1) * X, :] = c + 12.0 * DAMP

    lane = iota((FX, Y), 1)

    def one(i, carry):
        v = v_ref[i].reshape(FX, Y)
        hi, lo = split2(v)
        both = half_dot(w_hi[...], hi) + half_dot(w_lo[...], hi) + half_dot(w_hi[...], lo)
        u = both[FX:]
        out = both[:FX] + coeff[...] * v
        side = 4.0 * DAMP * v
        out = out + where0(lane < Y - 1, roll(u - side, -1, 1))
        out = out - where0(lane > 0, roll(u + side, 1, 1))
        two = DAMP * v
        out = out + where0(lane < Y - 2, roll(two, -2, 1)) + where0(lane > 1, roll(two, 2, 1))
        out_ref[i] = out.reshape(F, X, Y)
        return carry

    lax.fori_loop(0, step_m, one, 0)


def inside(v, along, across, coll, mask, types, rates, table, step_m=4):
    smem = pl.BlockSpec(memory_space=pltpu.SMEM)
    whole2 = lambda i: (0, 0)
    return pl.pallas_call(
        functools.partial(inside_kernel, step_m=step_m),
        grid=(M // step_m,),
        in_specs=[
            pl.BlockSpec((step_m, F, X, Y), lambda i: (i, 0, 0, 0)),
            pl.BlockSpec((F, F), whole2),
            pl.BlockSpec((F, F), whole2),
            pl.BlockSpec((X, Y), whole2),
            pl.BlockSpec((X, Y), whole2),
            pl.BlockSpec((X, Y), whole2),
            smem,
            smem,
        ],
        out_specs=pl.BlockSpec((step_m, F, X, Y), lambda i: (i, 0, 0, 0)),
        out_shape=jax.ShapeDtypeStruct((M, F, X, Y), F32),
        scratch_shapes=[
            pltpu.VMEM((2 * FX, FX), BF16),
            pltpu.VMEM((2 * FX, FX), BF16),
            pltpu.VMEM((FX, Y), F32),
        ],
        cost_estimate=pl.CostEstimate(
            flops=8 * 10**9, bytes_accessed=7 * 10**6, transcendentals=0
        ),
        name="inside",
    )(v, along, across, coll, mask, types, rates, table)


def diagonal(big, small, left, right):
    rows, cols = left * X, right * X
    own = iota((rows, cols), 0) % X == iota((rows, cols), 1) % X
    pick = (iota((cols, 128), 0) // X == iota((cols, 128), 1)).astype(F32)
    big = exact_dot(where0(own, big), pick)
    small = exact_dot(where0(own, small), pick)
    big, small = big.reshape(left, X, 128), small.reshape(left, X, 128)
    for shift in (4, 2, 1):
        big, err = two_sum(big, roll(big, shift, 1))
        small = small + roll(small, shift, 1) + err
    sel = (iota((left, rows), 1) == X * iota((left, rows), 0)).astype(F32)
    return exact_dot(sel, big.reshape(rows, 128)), exact_dot(sel, small.reshape(rows, 128))


def basis_kernel(p_ref, out_ref, acc, *, step_f):
    @pl.when(pl.program_id(0) == 0)
    def _():
        acc[...] = jnp.zeros_like(acc)

    def one(f, carry):
        hi, lo = split2(p_ref[:, f].reshape(KX, Y))
        both = jnp.concatenate([hi, lo], axis=0)
        acc[...] += half_dot(both, both, NT)
        return carry

    lax.fori_loop(0, step_f, one, 0)

    @pl.when(pl.program_id(0) == F // step_f - 1)
    def _():
        big = acc[0:KX, 0:KX]
        small = acc[0:KX, KX:] + acc[KX:, 0:KX] + acc[KX:, KX:]
        hi, lo = diagonal(big, small, K, K)
        lane = iota((8, 128), 1)
        for half, part in enumerate((hi, lo)):
            line = where0((lane >= 80) & (lane < 104), roll(part[0:8], 80, 1))
            line = line + where0((lane >= 104) & (lane < 120), roll(part[8:16], 96, 1))
            line = line + where0(lane >= 120, roll(part[16:24], 104, 1))
            out_ref[8 * half : 8 * half + 8, :] = line


def basis(p, step_f=13):
    return pl.pallas_call(
        functools.partial(basis_kernel, step_f=step_f),
        grid=(F // step_f,),
        in_specs=[pl.BlockSpec((K, step_f, X, Y), lambda i: (0, i, 0, 0))],
        out_specs=pl.BlockSpec((16, 128), lambda i: (0, 0)),
        out_shape=jax.ShapeDtypeStruct((16, 128), F32),
        scratch_shapes=[pltpu.VMEM((2 * KX, 2 * KX), F32)],
        cost_estimate=pl.CostEstimate(
            flops=8 * 10**9, bytes_accessed=5 * 10**6, transcendentals=0
        ),
        name="basis",
    )(p)


def halo_kernel(
    a_hbm, p_hbm, before_ref, after_ref, ybefore_ref, yafter_ref, along_ref, across_ref, gp_ref,
    out_hbm, line_ref, a, p, w_hi, w_lo, cb, ca, acc, sems,
):
    get_a = pltpu.make_async_copy(a_hbm, a, sems.at[0])
    get_p = pltpu.make_async_copy(p_hbm, p, sems.at[1])
    get_a.start()
    get_p.start()

    row, col = iota((FX, HALO), 0), iota((FX, HALO), 1)
    x, f = row % X, row // X
    g, j = col % (2 * F) // 2, col % 2
    left = (iota((FX, F), 0) // X == iota((FX, F), 1)).astype(F32)
    gcol = iota((F, HALO), 1) % (2 * F) // 2
    right = (gcol == iota((F, HALO), 0)).astype(F32)
    fa = 0.5 * exact_dot(exact_dot(left, along_ref[...]), right)
    same = f == g
    edge = (x == 0) & (j == 1)
    wb = where0(edge, -fa) + jnp.where(same & edge, -4.0 * DAMP, 0.0)
    wb = wb + jnp.where(same & (x == j), DAMP, 0.0)
    edge = (x == X - 1) & (j == 0)
    wa = where0(edge, fa) + jnp.where(same & edge, -4.0 * DAMP, 0.0)
    wa = wa + jnp.where(same & (x == X - 2 + j), DAMP, 0.0)
    w = jnp.concatenate([wb, wa], axis=1)
    owner = iota((FX, 2 * HALO), 1) % HALO // (2 * F)
    for i in range(2):
        hi, lo = split2(where0(owner == i, w))
        w_hi[i * FX : (i + 1) * FX, :] = hi
        w_lo[i * FX : (i + 1) * FX, :] = lo

    full = iota((FX, FX), 1) % X == iota((FX, FX), 0) % X
    wy = where0(full, 0.5 * spread(across_ref[...], FX, FX))
    lane = iota((FX, 128), 1)
    yb, ya = ybefore_ref[...], yafter_ref[...]
    term = exact_dot(wy, yb) + 4.0 * DAMP * yb
    cb[...] = DAMP * yb - where0(lane % 2 == 0, roll(term, -1, 1))
    term = exact_dot(wy, ya) - 4.0 * DAMP * ya
    ca[...] = DAMP * ya + where0(lane % 2 == 1, roll(term, 1, 1))

    get_a.wait()

    def pair(q, carry):
        h = jnp.concatenate([before_ref[q], after_ref[q]], axis=0)
        hi, lo = split2(h)
        both = half_dot(w_hi[...], hi) + half_dot(w_lo[...], hi) + half_dot(w_hi[...], lo)
        for i in range(2):
            m = 2 * q + i
            left = where0(lane < 2, roll(cb[...], (128 - 2 * m) % 128, 1))
            right = where0(lane >= 126, roll(ca[...], 126 - 2 * m, 1))
            part = a[m].reshape(FX, Y) + both[i * FX : (i + 1) * FX]
            part = part + jnp.concatenate([left, right], axis=1)
            a[m] = part.reshape(F, X, Y)
        return carry

    lax.fori_loop(0, PAIRS, pair, 0)
    put = pltpu.make_async_copy(a, out_hbm, sems.at[2])
    put.start()
    get_p.wait()
    acc[...] = jnp.zeros_like(acc)

    def field(f, carry):
        a_hi, a_lo = split2(a[:, f].reshape(MX, Y))
        p_hi, p_lo = split2(p[:, f].reshape(KX, Y))
        rows = jnp.concatenate([p_hi, a_hi, p_lo, a_lo], axis=0)
        cols = jnp.concatenate([a_hi, a_lo], axis=0)
        acc[...] += half_dot(rows, cols, NT)
        return carry

    lax.fori_loop(0, F, field, 0)
    n = KX + MX
    big = acc[0:n, 0:MX]
    small = acc[0:n, MX:] + acc[n:, 0:MX] + acc[n:, MX:]
    hi, lo = diagonal(big, small, K + M, M)
    lane = iota((8, 128), 1)
    for half, part in enumerate((hi, lo)):
        line = gp_ref[8 * half : 8 * half + 8, :]
        for i in range((K + M) // 8):
            mine = (lane >= 16 * i) & (lane < 16 * i + 16)
            line = line + where0(mine, roll(part[8 * i : 8 * i + 8], 16 * i, 1))
        for copy in range(line_ref.shape[0]):
            line_ref[copy, 8 * half : 8 * half + 8, :] = line
    put.wait()


def with_halo(a, p, before, after, ybefore, yafter, along, across, gp, copies):
    vmem = pl.BlockSpec(memory_space=pltpu.VMEM)
    anywhere = pl.BlockSpec(memory_space=pl.ANY)
    return pl.pallas_call(
        halo_kernel,
        in_specs=[anywhere, anywhere] + [vmem] * 7,
        out_specs=[anywhere, vmem],
        out_shape=[
            jax.ShapeDtypeStruct((M, F, X, Y), F32),
            jax.ShapeDtypeStruct((copies, 16, 128), F32),
        ],
        scratch_shapes=[
            pltpu.VMEM((M, F, X, Y), F32),
            pltpu.VMEM((K, F, X, Y), F32),
            pltpu.VMEM((2 * FX, 2 * HALO), BF16),
            pltpu.VMEM((2 * FX, 2 * HALO), BF16),
            pltpu.VMEM((FX, 128), F32),
            pltpu.VMEM((FX, 128), F32),
            pltpu.VMEM((2 * (KX + MX), 2 * MX), F32),
            pltpu.SemaphoreType.DMA((3,)),
        ],
        cost_estimate=pl.CostEstimate(
            flops=8 * 10**9, bytes_accessed=14 * 10**6, transcendentals=0
        ),
        name="halo",
    )(a, p, before, after, ybefore, yafter, along, across, gp)


def pair_total(ref):
    hi, lo = ref[0, 0:8, :], ref[0, 8:16, :]
    for i in range(1, ref.shape[0]):
        hi, err = two_sum(hi, ref[i, 0:8, :])
        lo = lo + ref[i, 8:16, :] + err
    return hi, lo


def middle_kernel(in_ref, out_ref):
    hi, lo = pair_total(in_ref)
    hi, lo = two_sum(hi, lo)
    for i in range(out_ref.shape[0]):
        out_ref[i, 0:8, :] = hi
        out_ref[i, 8:16, :] = lo


def middle(lines, copies):
    return pl.pallas_call(
        middle_kernel,
        out_shape=jax.ShapeDtypeStruct((copies, 16, 128), F32),
        name="middle",
    )(lines)


def sent_to_all(copies, axis):
    return lax.all_to_all(copies, axis, split_axis=0, concat_axis=0, tiled=True)


def grid_of(v, top):
    return (v + top) - top


def slices(hi, lo, axis):
    top = jnp.max(jnp.abs(hi), axis=axis, keepdims=True)
    first = grid_of(hi, top * 2.0**16)
    rest = hi - first
    second = grid_of(rest, top * 2.0**8)
    return first, second, (rest - second) + lo


def pair_dot(a, b, dims):
    a1, a2, a3 = slices(*a, dims[0][0][0])
    b1, b2, b3 = slices(*b, dims[0][1][0])
    dot = functools.partial(exact_dot, dims=dims)
    big = dot(a1, b1)
    mid = dot(a1, b2) + dot(a2, b1)
    low = dot(a1, b3) + dot(a2, b2 + b3) + dot(a3, b1 + b2)
    big, err = two_sum(big, mid)
    return two_sum(big, err + low)


def pair_add(a, b):
    big, err = two_sum(a[0], b[0])
    return two_sum(big, err + (a[1] + b[1]))


def factor(gram):
    n = gram.shape[0]
    row, lane = iota((n, 128), 0), iota((n, 128), 1)
    eye = (iota((n, n), 0) == iota((n, n), 1)).astype(F32)
    t = jnp.concatenate([gram, eye, jnp.zeros((n, 128 - 2 * n), F32)], axis=1)
    pivots = jnp.zeros((n, 128), F32)
    for k in range(n):
        column = jnp.broadcast_to(t[:, k : k + 1], (n, 128))
        pivot = jnp.broadcast_to(column[k : k + 1, :], (n, 128))
        line = jnp.broadcast_to(t[k : k + 1, :], (n, 128))
        pivots = jnp.where(row == k, pivot, pivots)
        t = t - where0(row > k, column / pivot) * line
    t = t / jnp.sqrt(pivots)
    upper = where0(row <= lane, t)[:, 0:n]
    return upper, t[:, n : 2 * n]


def final_kernel(
    line_ref, a_hbm, p_hbm, out_hbm, proj_ref, tri_ref,
    a, p, out, ma, mp, in_sems, out_sems, *, cells, parts,
):
    size = F // parts
    gets = []
    for i in range(parts):
        part = pl.ds(i * size, size)
        gets.append(
            (
                pltpu.make_async_copy(a_hbm.at[:, part], a.at[:, part], in_sems.at[0, i]),
                pltpu.make_async_copy(p_hbm.at[:, part], p.at[:, part], in_sems.at[1, i]),
            )
        )
        for get in gets[-1]:
            get.start()

    hi, lo = pair_total(line_ref)
    hi, lo = two_sum(hi, lo)
    odd = cells
    while odd % 2 == 0:
        odd //= 2
    scale = float(odd) / float(cells)
    guess = hi / float(odd)
    big = guess * 4097.0
    big = big - (big - guess)
    left = ((hi - big * float(odd)) - (guess - big) * float(odd)) + lo
    hi, lo = two_sum(guess, left / float(odd))
    hi, lo = hi * scale, lo * scale

    lane8 = iota((8, 128), 1)

    def unpack(v):
        rows = [roll(v, -16 * i, 1) for i in range(5)]
        top = where0(lane8 < 24, roll(v, -80, 1))
        centre = where0((lane8 >= 8) & (lane8 < 24), roll(v, -96, 1))
        end = where0((lane8 >= 16) & (lane8 < 24), roll(v, -104, 1))
        upper = jnp.concatenate([top, centre, end], axis=0)[:, 0:K]
        off = where0(iota((K, K), 1) // 8 > iota((K, K), 0) // 8, upper)
        eye = (iota((K, K), 0) == iota((K, K), 1)).astype(F32)
        return (
            jnp.concatenate(rows[0:3], axis=0)[:, 0:M],
            jnp.concatenate(rows[3:5], axis=0)[:, 0:M],
            upper + exact_dot(eye, off, NT),
        )

    (c_hi, s_hi, g_hi), (c_lo, s_lo, g_lo) = unpack(hi), unpack(lo)
    zero = jnp.zeros((K, M), F32)
    second = c_hi - exact_dot(g_hi, c_hi)
    proj = c_hi + second
    proj_ref[...] = proj
    gp = pair_dot((g_hi, g_lo), (proj, zero), NN)
    t_hi, t_lo = pair_add(gp, (-c_hi, -c_lo))
    gram = pair_dot(
        (jnp.concatenate([proj, c_hi], axis=0), jnp.concatenate([zero, c_lo], axis=0)),
        (jnp.concatenate([t_hi, -proj], axis=0), jnp.concatenate([t_lo, zero], axis=0)),
        TN,
    )
    gram = pair_add((s_hi, s_lo), gram)
    upper_one, inv_one = factor(gram[0])
    none = jnp.zeros((M, M), F32)
    again = pair_dot((inv_one, none), gram, NN)
    again = pair_dot(again, (inv_one, none), NT)
    upper_two, inv_two = factor(again[0] + again[1])
    tri_ref[...] = exact_dot(upper_two, upper_one)
    mix = exact_dot(inv_two, inv_one)
    mix_p = -exact_dot(mix, proj, NT)

    row, col = iota((MX, MX), 0), iota((MX, MX), 1)
    m1, m2, m3 = split3(where0(row % X == col % X, spread(mix, MX, MX)))
    ma[0] = jnp.concatenate([m1, m1], axis=1)
    ma[1] = jnp.concatenate([m2, m2], axis=1)
    ma[2] = jnp.concatenate([m3, jnp.zeros_like(m3)], axis=1)
    row, col = iota((MX, KX), 0), iota((MX, KX), 1)
    n1, n2 = split2(where0(row % X == col % X, spread(mix_p, MX, KX)))
    mp[0] = n1
    mp[1] = n2

    def field(f, carry):
        a1, a2, a3 = split3(a[:, f].reshape(MX, Y))
        p1, p2 = split2(p[:, f].reshape(KX, Y))
        both = jnp.concatenate([a1, a2], axis=0)
        total = half_dot(mp[0], p2) + half_dot(mp[1], p1) + half_dot(ma[2], both)
        total = total + half_dot(ma[0][:, 0:MX], a3) + half_dot(ma[1], both)
        total = total + half_dot(mp[0], p1) + half_dot(ma[0], both)
        out[:, f] = total.reshape(M, X, Y)
        return carry

    puts = []
    for i in range(parts):
        for get in gets[i]:
            get.wait()
        lax.fori_loop(i * size, (i + 1) * size, field, 0)
        part = pl.ds(i * size, size)
        puts.append(pltpu.make_async_copy(out.at[:, part], out_hbm.at[:, part], out_sems.at[i]))
        puts[-1].start()
    for put in puts:
        put.wait()


def final(lines, a, p, cells, parts=2):
    vmem = pl.BlockSpec(memory_space=pltpu.VMEM)
    anywhere = pl.BlockSpec(memory_space=pl.ANY)
    return pl.pallas_call(
        functools.partial(final_kernel, cells=cells, parts=parts),
        in_specs=[vmem, anywhere, anywhere],
        out_specs=[anywhere, vmem, vmem],
        out_shape=[
            jax.ShapeDtypeStruct((M, F, X, Y), F32),
            jax.ShapeDtypeStruct((K, M), F32),
            jax.ShapeDtypeStruct((M, M), F32),
        ],
        scratch_shapes=[
            pltpu.VMEM((M, F, X, Y), F32),
            pltpu.VMEM((K, F, X, Y), F32),
            pltpu.VMEM((M, F, X, Y), F32),
            pltpu.VMEM((3, MX, 2 * MX), BF16),
            pltpu.VMEM((2, MX, KX), BF16),
            pltpu.SemaphoreType.DMA((2, parts)),
            pltpu.SemaphoreType.DMA((parts,)),
        ],
        name="final",
    )(lines, a, p)


def on_device(
    krylov_block, prior_basis, flux_along, flux_across, collision, field_rates, wall_table,
    wall_mask, wall_type,
):
    cells = F * X * lax.axis_size(GX) * Y * lax.axis_size(GY)
    first, last, yfirst, ylast = pack(krylov_block)

    def onward(axis):
        return [(i, i + 1) for i in range(lax.axis_size(axis) - 1)]

    def back(axis):
        return [(j, i) for i, j in onward(axis)]

    before = lax.ppermute(last, GX, onward(GX))
    after = lax.ppermute(first, GX, back(GX))
    ybefore = lax.ppermute(ylast, GY, onward(GY))
    yafter = lax.ppermute(yfirst, GY, back(GY))
    applied = inside(
        krylov_block, flux_along, flux_across, collision, wall_mask, wall_type, field_rates,
        wall_table,
    )
    gp = basis(prior_basis)
    sizes = [lax.axis_size(stage) for stage in STAGES]
    applied, lines = with_halo(
        applied, prior_basis, before, after, ybefore, yafter, flux_along, flux_across, gp, sizes[0]
    )
    lines = middle(sent_to_all(lines, STAGES[0]), sizes[1])
    lines = sent_to_all(lines, STAGES[1])
    return final(lines, applied, prior_basis, cells)


def solution(mesh):
    torus = Mesh(mesh.devices.reshape(8, 4, 4, 2), ("gx_z", "gx_x", "gy_y", "gy_c"))
    cells = P(GX, GY)
    stack = P(None, None, GX, GY)
    in_specs = (stack, stack, P(), P(), cells, P(), P(), cells, cells)
    out_specs = (stack, P(), P())
    return jax.shard_map(
        on_device, mesh=torus, in_specs=in_specs, out_specs=out_specs, check_vma=False
    )
```

```python
import functools

import jax
import jax.numpy as jnp
from jax import lax
from jax.experimental import pallas as pl
from jax.experimental.pallas import tpu as pltpu
from jax.sharding import Mesh
from jax.sharding import PartitionSpec as P

GX = ("gx_z", "gx_x")
GY = ("gy_y", "gy_c")
STAGES = (("gx_x", "gy_y"), ("gx_z", "gy_c"))

DAMP = 0.0625
PRECISE = lax.Precision.HIGHEST
F32 = jnp.float32
BF16 = jnp.bfloat16

M = 16
K = 24
F = 26
X = 8
Y = 256
FX = F * X
MX = M * X
KX = K * X
PAIRS = M // 2
HALO = 4 * F

NN = (((1,), (0,)), ((), ()))
NT = (((1,), (1,)), ((), ()))
TN = (((0,), (0,)), ((), ()))


def exact_dot(a, b, dims=NN):
    return lax.dot_general(a, b, dims, precision=PRECISE, preferred_element_type=F32)


def half_dot(a, b, dims=NN):
    return lax.dot_general(a, b, dims, preferred_element_type=F32)


def split2(v):
    hi = v.astype(BF16)
    return hi, (v - hi.astype(F32)).astype(BF16)


def split3(v):
    hi = v.astype(BF16)
    rest = v - hi.astype(F32)
    mid = rest.astype(BF16)
    return hi, mid, (rest - mid.astype(F32)).astype(BF16)


def iota(shape, dim):
    return lax.broadcasted_iota(jnp.int32, shape, dim)


def where0(mask, v):
    return jnp.where(mask, v, jnp.zeros_like(v))


def spread(small, rows, cols):
    n, k = small.shape
    left = (iota((rows, n), 0) // X == iota((rows, n), 1)).astype(F32)
    right = (iota((k, cols), 1) // X == iota((k, cols), 0)).astype(F32)
    return exact_dot(exact_dot(left, small), right)


def two_sum(a, b):
    s = a + b
    t = s - a
    return s, (a - (s - t)) + (b - t)


def roll(v, shift, axis):
    size = v.shape[axis]
    return pltpu.roll(v, shift % size if isinstance(shift, int) else shift, axis)


def pack_kernel(v_ref, first_ref, last_ref, *, step_m):
    for i in range(step_m):
        for f in range(F):
            at = (i % 2 * F + f) * 2
            first_ref[i // 2, at : at + 2, :] = v_ref[i, f, 0:2, :]
            last_ref[i // 2, at : at + 2, :] = v_ref[i, f, X - 2 : X, :]


def pack(v, step_m=4):
    return pl.pallas_call(
        functools.partial(pack_kernel, step_m=step_m),
        grid=(M // step_m,),
        in_specs=[pl.BlockSpec((step_m, F, X, Y), lambda i: (i, 0, 0, 0))],
        out_specs=[pl.BlockSpec((step_m // 2, HALO, Y), lambda i: (i, 0, 0))] * 2,
        out_shape=[jax.ShapeDtypeStruct((PAIRS, HALO, Y), F32)] * 2,
        cost_estimate=pl.CostEstimate(flops=10**6, bytes_accessed=6 * 10**6, transcendentals=0),
        name="pack",
    )(v)


def inside_kernel(
    v_ref, along_ref, across_ref, coll_ref, mask_ref, type_ref, rate_ref, table_ref,
    out_ref, yfirst_ref, ylast_ref, halo_ref, w, coeff, *, step_m,
):
    @pl.when(pl.program_id(0) == 0)
    def _():
        row, col = iota((FX, FX), 0), iota((FX, FX), 1)
        same_f = row // X == col // X
        step = col % X - row % X
        fa = spread(along_ref[...], FX, FX)
        fc = spread(across_ref[...], FX, FX)
        wx = where0(step == 1, 0.5 * fa) - where0(step == -1, 0.5 * fa)
        near = same_f & (jnp.abs(step) == 1)
        far = same_f & (jnp.abs(step) == 2)
        wx = wx + jnp.where(near, -4.0 * DAMP, 0.0) + jnp.where(far, DAMP, 0.0)
        wy = where0(step == 0, 0.5 * fc)
        for i, part in enumerate((wx, wy)):
            hi, lo = split2(part)
            w[0, i * FX : (i + 1) * FX, :] = hi
            w[1, i * FX : (i + 1) * FX, :] = lo
        walls = [
            jnp.where(type_ref[...] == t, mask_ref[...].astype(F32), 0.0)
            for t in range(table_ref.shape[0])
        ]
        for f in range(F):
            c = coll_ref[...] * rate_ref[f]
            for t, wall in enumerate(walls):
                c = c + wall * table_ref[t, f]
            coeff[f * X : (f + 1) * X, :] = c + 12.0 * DAMP

        row, col = iota((FX, HALO), 0), iota((FX, HALO), 1)
        x, f = row % X, row // X
        g, j, later = col % (2 * F) // 2, col % 2, col >= 2 * F
        left = (iota((FX, F), 0) // X == iota((FX, F), 1)).astype(F32)
        right = (iota((F, HALO), 1) % (2 * F) // 2 == iota((F, HALO), 0)).astype(F32)
        fa = 0.5 * exact_dot(exact_dot(left, along_ref[...]), right)
        same = f == g
        edge_b = (x == 0) & (j == 1) & ~later
        edge_a = (x == X - 1) & (j == 0) & later
        wh = where0(edge_a, fa) - where0(edge_b, fa)
        wh = wh + jnp.where(same & (edge_a | edge_b), -4.0 * DAMP, 0.0)
        outer = ((x == j) & ~later) | ((x == X - 2 + j) & later)
        wh = wh + jnp.where(same & outer, DAMP, 0.0)
        hi = wh.astype(BF16).astype(F32)
        halo_ref[0] = jnp.concatenate([hi, hi], axis=1).astype(BF16)
        halo_ref[1] = jnp.concatenate([wh - hi, jnp.zeros_like(wh)], axis=1).astype(BF16)
        yfirst_ref[...] = jnp.zeros_like(yfirst_ref)
        ylast_ref[...] = jnp.zeros_like(ylast_ref)

    lane = iota((FX, Y), 1)
    lane2 = iota((FX, 128), 1) // 2

    def one(i, carry):
        m = pl.program_id(0) * step_m + i
        v = v_ref[i].reshape(FX, Y)
        mine = lane2 == m
        yfirst_ref[...] = jnp.where(mine, roll(v[:, 0:128], 2 * m, 1), yfirst_ref[...])
        ylast_ref[...] = jnp.where(mine, roll(v[:, Y - 128 :], 2 * m + 2, 1), ylast_ref[...])
        hi, lo = split2(v)
        left = jnp.concatenate([w[0], w[1], w[0]], axis=1)
        both = half_dot(left, jnp.concatenate([hi, hi, lo], axis=0))
        u = both[FX:]
        out = both[:FX] + coeff[...] * v
        side = 4.0 * DAMP * v
        out = out + where0(lane < Y - 1, roll(u - side, -1, 1))
        out = out - where0(lane > 0, roll(u + side, 1, 1))
        two = DAMP * v
        out = out + where0(lane < Y - 2, roll(two, -2, 1)) + where0(lane > 1, roll(two, 2, 1))
        out_ref[i] = out.reshape(F, X, Y)
        return carry

    lax.fori_loop(0, step_m, one, 0)


def inside(v, along, across, coll, mask, types, rates, table, step_m=4):
    smem = pl.BlockSpec(memory_space=pltpu.SMEM)
    whole2 = lambda i: (0, 0)
    return pl.pallas_call(
        functools.partial(inside_kernel, step_m=step_m),
        grid=(M // step_m,),
        in_specs=[
            pl.BlockSpec((step_m, F, X, Y), lambda i: (i, 0, 0, 0)),
            pl.BlockSpec((F, F), whole2),
            pl.BlockSpec((F, F), whole2),
            pl.BlockSpec((X, Y), whole2),
            pl.BlockSpec((X, Y), whole2),
            pl.BlockSpec((X, Y), whole2),
            smem,
            smem,
        ],
        out_specs=[
            pl.BlockSpec((step_m, F, X, Y), lambda i: (i, 0, 0, 0)),
            pl.BlockSpec((FX, 128), whole2),
            pl.BlockSpec((FX, 128), whole2),
            pl.BlockSpec((2, FX, 2 * HALO), lambda i: (0, 0, 0)),
        ],
        out_shape=[
            jax.ShapeDtypeStruct((M, F, X, Y), F32),
            jax.ShapeDtypeStruct((FX, 128), F32),
            jax.ShapeDtypeStruct((FX, 128), F32),
            jax.ShapeDtypeStruct((2, FX, 2 * HALO), BF16),
        ],
        scratch_shapes=[pltpu.VMEM((2, 2 * FX, FX), BF16), pltpu.VMEM((FX, Y), F32)],
        cost_estimate=pl.CostEstimate(
            flops=8 * 10**9, bytes_accessed=7 * 10**6, transcendentals=0
        ),
        name="inside",
    )(v, along, across, coll, mask, types, rates, table)


def columns_kernel(ybefore_ref, yafter_ref, across_ref, cb_ref, ca_ref):
    full = iota((FX, FX), 1) % X == iota((FX, FX), 0) % X
    wy = where0(full, 0.5 * spread(across_ref[...], FX, FX))
    lane = iota((FX, 128), 1)
    yb, ya = ybefore_ref[...], yafter_ref[...]
    term = exact_dot(wy, yb) + 4.0 * DAMP * yb
    cb_ref[...] = DAMP * yb - where0(lane % 2 == 0, roll(term, -1, 1))
    term = exact_dot(wy, ya) - 4.0 * DAMP * ya
    ca_ref[...] = DAMP * ya + where0(lane % 2 == 1, roll(term, 1, 1))


def columns(ybefore, yafter, across):
    return pl.pallas_call(
        columns_kernel,
        out_shape=[jax.ShapeDtypeStruct((FX, 128), F32)] * 2,
        cost_estimate=pl.CostEstimate(flops=10**8, bytes_accessed=10**6, transcendentals=0),
        name="columns",
    )(ybefore, yafter, across)


def diagonal(big, small, left, right):
    rows, cols = left * X, right * X
    own = iota((rows, cols), 0) % X == iota((rows, cols), 1) % X
    pick = (iota((cols, 128), 0) // X == iota((cols, 128), 1)).astype(F32)
    big = exact_dot(where0(own, big), pick)
    small = exact_dot(where0(own, small), pick)
    big, small = big.reshape(left, X, 128), small.reshape(left, X, 128)
    for shift in (4, 2, 1):
        big, err = two_sum(big, roll(big, shift, 1))
        small = small + roll(small, shift, 1) + err
    sel = (iota((left, rows), 1) == X * iota((left, rows), 0)).astype(F32)
    return exact_dot(sel, big.reshape(rows, 128)), exact_dot(sel, small.reshape(rows, 128))


TWO = F // 2


def basis_kernel(p_hbm, out_ref, hi_hbm, lo_hbm, p, hi_ref, lo_ref, big_ref, small_ref, in_sem, out_sem):
    def get(q):
        return pltpu.make_async_copy(
            p_hbm.at[:, pl.ds(2 * q, 2)], p.at[:, pl.ds(2 * q, 2)], in_sem.at[q]
        )

    def puts(q):
        at = pl.ds(2 * q, 2)
        return (
            pltpu.make_async_copy(hi_ref.at[at], hi_hbm.at[at], out_sem.at[0, q]),
            pltpu.make_async_copy(lo_ref.at[at], lo_hbm.at[at], out_sem.at[1, q]),
        )

    for q in range(TWO):
        get(q).start()
    big_ref[...] = jnp.zeros_like(big_ref)
    small_ref[...] = jnp.zeros_like(small_ref)

    def two(q, carry):
        get(q).wait()
        his, los = [], []
        for i in range(2):
            hi, lo = split2(p[:, 2 * q + i].reshape(KX, Y))
            hi_ref[2 * q + i] = hi
            lo_ref[2 * q + i] = lo
            his.append(hi)
            los.append(lo)
        hi = jnp.concatenate(his, axis=1)
        lo = jnp.concatenate(los, axis=1)
        for put in puts(q):
            put.start()
        big_ref[...] += half_dot(hi, hi, NT)
        half = lo * jnp.asarray(0.5, BF16)
        small_ref[...] += half_dot(
            jnp.concatenate([lo, lo], axis=1), jnp.concatenate([hi, half], axis=1), NT
        )
        return carry

    lax.fori_loop(0, TWO, two, 0)
    hi, lo = diagonal(big_ref[...], small_ref[...], K, K)
    eye = (iota((K, K), 0) == iota((K, 128), 1)[:, 0:K]).astype(F32)
    turned = exact_dot(lo[:, 0:K], eye, TN)
    lo = lo + jnp.concatenate([turned, jnp.zeros((K, 128 - K), F32)], axis=1)
    lane = iota((8, 128), 1)
    for half, part in enumerate((hi, lo)):
        line = where0((lane >= 80) & (lane < 104), roll(part[0:8], 80, 1))
        line = line + where0((lane >= 104) & (lane < 120), roll(part[8:16], 96, 1))
        line = line + where0(lane >= 120, roll(part[16:24], 104, 1))
        out_ref[8 * half : 8 * half + 8, :] = line

    def end(q, carry):
        for put in puts(q):
            put.wait()
        return carry

    lax.fori_loop(0, TWO, end, 0)


def basis(p):
    anywhere = pl.BlockSpec(memory_space=pl.ANY)
    return pl.pallas_call(
        basis_kernel,
        in_specs=[anywhere],
        out_specs=[pl.BlockSpec(memory_space=pltpu.VMEM), anywhere, anywhere],
        out_shape=[
            jax.ShapeDtypeStruct((16, 128), F32),
            jax.ShapeDtypeStruct((F, KX, Y), BF16),
            jax.ShapeDtypeStruct((F, KX, Y), BF16),
        ],
        scratch_shapes=[
            pltpu.VMEM((K, F, X, Y), F32),
            pltpu.VMEM((F, KX, Y), BF16),
            pltpu.VMEM((F, KX, Y), BF16),
            pltpu.VMEM((KX, KX), F32),
            pltpu.VMEM((KX, KX), F32),
            pltpu.SemaphoreType.DMA((TWO,)),
            pltpu.SemaphoreType.DMA((2, TWO)),
        ],
        cost_estimate=pl.CostEstimate(
            flops=8 * 10**9, bytes_accessed=10 * 10**6, transcendentals=0
        ),
        name="basis",
    )(p)


def halo_kernel(
    a_hbm, hi_hbm, lo_hbm, before_hbm, after_hbm, cb_ref, ca_ref, w_ref, gp_ref,
    out_hbm, line_ref, a, p_hi, p_lo, before, after, acc, a_sem, sems,
):
    def get(q):
        at = pl.ds(2 * q, 2)
        return (
            pltpu.make_async_copy(a_hbm.at[at], a.at[at], a_sem.at[0, q]),
            pltpu.make_async_copy(before_hbm.at[q], before.at[q], a_sem.at[1, q]),
            pltpu.make_async_copy(after_hbm.at[q], after.at[q], a_sem.at[2, q]),
        )

    def put(q):
        at = pl.ds(2 * q, 2)
        return pltpu.make_async_copy(a.at[at], out_hbm.at[at], a_sem.at[3, q])

    get_hi = pltpu.make_async_copy(hi_hbm, p_hi, sems.at[0])
    get_lo = pltpu.make_async_copy(lo_hbm, p_lo, sems.at[1])
    for q in range(PAIRS):
        for each in get(q):
            each.start()
    get_hi.start()
    get_lo.start()
    lane = iota((FX, 128), 1)

    def pair(q, carry):
        for each in get(q):
            each.wait()
        for i in range(2):
            m = 2 * q + i
            mine = slice(i * 2 * F, (i + 1) * 2 * F)
            h = jnp.concatenate([before[q][mine], after[q][mine]], axis=0)
            hi = h.astype(BF16).astype(F32)
            h = jnp.concatenate([hi, h - hi], axis=0).astype(BF16)
            left = where0(lane < 2, roll(cb_ref[...], (128 - 2 * m) % 128, 1))
            right = where0(lane >= 126, roll(ca_ref[...], 126 - 2 * m, 1))
            part = a[m].reshape(FX, Y) + jnp.concatenate([left, right], axis=1)
            part = part + (half_dot(w_ref[0], h) + half_dot(w_ref[1], h))
            a[m] = part.reshape(F, X, Y)
        put(q).start()
        return carry

    lax.fori_loop(0, PAIRS, pair, 0)
    acc[...] = jnp.zeros_like(acc)
    get_hi.wait()
    get_lo.wait()

    def two(q, carry):
        his, los, p_his, p_los = [], [], [], []
        for i in range(2):
            hi, lo = split2(a[:, 2 * q + i].reshape(MX, Y))
            his.append(hi)
            los.append(lo)
            p_his.append(p_hi[2 * q + i])
            p_los.append(p_lo[2 * q + i])
        hi, lo, ph, pl_ = (jnp.concatenate(v, axis=1) for v in (his, los, p_his, p_los))
        rows = jnp.concatenate([ph, hi, pl_, lo], axis=0)
        acc[...] += half_dot(rows, jnp.concatenate([hi, lo], axis=0), NT)
        return carry

    lax.fori_loop(0, TWO, two, 0)
    n = KX + MX
    big = acc[0:n, 0:MX]
    small = acc[0:n, MX:] + acc[n:, 0:MX] + acc[n:, MX:]
    hi, lo = diagonal(big, small, K + M, M)
    lane = iota((8, 128), 1)
    for half, part in enumerate((hi, lo)):
        line = gp_ref[8 * half : 8 * half + 8, :]
        for i in range((K + M) // 8):
            mine = (lane >= 16 * i) & (lane < 16 * i + 16)
            line = line + where0(mine, roll(part[8 * i : 8 * i + 8], 16 * i, 1))
        for copy in range(line_ref.shape[0]):
            line_ref[copy, 8 * half : 8 * half + 8, :] = line

    def end(q, carry):
        put(q).wait()
        return carry

    lax.fori_loop(0, PAIRS, end, 0)


def with_halo(a, p_hi, p_lo, before, after, cb, ca, weights, gp, copies):
    vmem = pl.BlockSpec(memory_space=pltpu.VMEM)
    anywhere = pl.BlockSpec(memory_space=pl.ANY)
    return pl.pallas_call(
        halo_kernel,
        in_specs=[anywhere] * 5 + [vmem] * 4,
        out_specs=[anywhere, vmem],
        out_shape=[
            jax.ShapeDtypeStruct((M, F, X, Y), F32),
            jax.ShapeDtypeStruct((copies, 16, 128), F32),
        ],
        scratch_shapes=[
            pltpu.VMEM((M, F, X, Y), F32),
            pltpu.VMEM((F, KX, Y), BF16),
            pltpu.VMEM((F, KX, Y), BF16),
            pltpu.VMEM((PAIRS, HALO, Y), F32),
            pltpu.VMEM((PAIRS, HALO, Y), F32),
            pltpu.VMEM((2 * (KX + MX), 2 * MX), F32),
            pltpu.SemaphoreType.DMA((4, PAIRS)),
            pltpu.SemaphoreType.DMA((2,)),
        ],
        cost_estimate=pl.CostEstimate(
            flops=8 * 10**9, bytes_accessed=14 * 10**6, transcendentals=0
        ),
        name="halo",
    )(a, p_hi, p_lo, before, after, cb, ca, weights, gp)


def pair_total(ref):
    hi, lo = ref[0, 0:8, :], ref[0, 8:16, :]
    for i in range(1, ref.shape[0]):
        hi, err = two_sum(hi, ref[i, 0:8, :])
        lo = lo + ref[i, 8:16, :] + err
    return hi, lo


def middle_kernel(in_ref, out_ref):
    hi, lo = pair_total(in_ref)
    hi, lo = two_sum(hi, lo)
    for i in range(out_ref.shape[0]):
        out_ref[i, 0:8, :] = hi
        out_ref[i, 8:16, :] = lo


def middle(lines, copies):
    return pl.pallas_call(
        middle_kernel,
        out_shape=jax.ShapeDtypeStruct((copies, 16, 128), F32),
        name="middle",
    )(lines)


def sent_to_all(copies, axis):
    return lax.all_to_all(copies, axis, split_axis=0, concat_axis=0, tiled=True)


def grid_of(v, top):
    return (v + top) - top


def slices(hi, lo, axis):
    top = jnp.max(jnp.abs(hi), axis=axis, keepdims=True)
    first = grid_of(hi, top * 2.0**16)
    rest = hi - first
    second = grid_of(rest, top * 2.0**8)
    return first, second, (rest - second) + lo


def pair_dot(a, b, dims):
    a1, a2, a3 = slices(*a, dims[0][0][0])
    b1, b2, b3 = slices(*b, dims[0][1][0])
    dot = functools.partial(exact_dot, dims=dims)
    big = dot(a1, b1)
    mid = dot(a1, b2) + dot(a2, b1)
    low = dot(a1, b3) + dot(a2, b2 + b3) + dot(a3, b1 + b2)
    big, err = two_sum(big, mid)
    return two_sum(big, err + low)


def pair_add(a, b):
    big, err = two_sum(a[0], b[0])
    return two_sum(big, err + (a[1] + b[1]))


def factor(gram):
    n = gram.shape[0]
    row, lane = iota((n, 128), 0), iota((n, 128), 1)
    eye = (iota((n, n), 0) == iota((n, n), 1)).astype(F32)
    t = jnp.concatenate([gram, eye, jnp.zeros((n, 128 - 2 * n), F32)], axis=1)
    pivots = jnp.zeros((n, 128), F32)
    for k in range(n):
        column = jnp.broadcast_to(t[:, k : k + 1], (n, 128))
        pivot = jnp.broadcast_to(column[k : k + 1, :], (n, 128))
        line = jnp.broadcast_to(t[k : k + 1, :], (n, 128))
        pivots = jnp.where(row == k, pivot, pivots)
        t = t - where0(row > k, column / pivot) * line
    t = t / jnp.sqrt(pivots)
    upper = where0(row <= lane, t)[:, 0:n]
    return upper, t[:, n : 2 * n]


def final_kernel(
    line_ref, a_hbm, hi_hbm, lo_hbm, out_hbm, proj_ref, tri_ref,
    a, p_hi, p_lo, out, table, mp, in_sems, out_sems, *, cells,
):
    gets = [
        pltpu.make_async_copy(src, dst, in_sems.at[i])
        for i, (src, dst) in enumerate(((a_hbm, a), (hi_hbm, p_hi), (lo_hbm, p_lo)))
    ]
    for get in gets:
        get.start()

    hi, lo = pair_total(line_ref)
    hi, lo = two_sum(hi, lo)
    odd = cells
    while odd % 2 == 0:
        odd //= 2
    scale = float(odd) / float(cells)
    guess = hi / float(odd)
    big = guess * 4097.0
    big = big - (big - guess)
    left = ((hi - big * float(odd)) - (guess - big) * float(odd)) + lo
    hi, lo = two_sum(guess, left / float(odd))
    hi, lo = hi * scale, lo * scale

    lane8 = iota((8, 128), 1)

    def unpack(v):
        rows = [roll(v, -16 * i, 1) for i in range(5)]
        top = where0(lane8 < 24, roll(v, -80, 1))
        centre = where0((lane8 >= 8) & (lane8 < 24), roll(v, -96, 1))
        end = where0((lane8 >= 16) & (lane8 < 24), roll(v, -104, 1))
        upper = jnp.concatenate([top, centre, end], axis=0)[:, 0:K]
        off = where0(iota((K, K), 1) // 8 > iota((K, K), 0) // 8, upper)
        eye = (iota((K, K), 0) == iota((K, K), 1)).astype(F32)
        return (
            jnp.concatenate(rows[0:3], axis=0)[:, 0:M],
            jnp.concatenate(rows[3:5], axis=0)[:, 0:M],
            upper + exact_dot(eye, off, NT),
        )

    (c_hi, s_hi, g_hi), (c_lo, s_lo, g_lo) = unpack(hi), unpack(lo)
    zero = jnp.zeros((K, M), F32)
    second = c_hi - exact_dot(g_hi, c_hi)
    proj = c_hi + second
    eye = (iota((K, K), 0) == iota((K, K), 1)).astype(F32)
    proj_ref[...] = exact_dot(proj, eye, TN)
    gp = pair_dot((g_hi, g_lo), (proj, zero), NN)
    t_hi, t_lo = pair_add(gp, (-c_hi, -c_lo))
    gram = pair_dot(
        (jnp.concatenate([proj, c_hi], axis=0), jnp.concatenate([zero, c_lo], axis=0)),
        (jnp.concatenate([t_hi, -proj], axis=0), jnp.concatenate([t_lo, zero], axis=0)),
        TN,
    )
    gram = pair_add((s_hi, s_lo), gram)
    upper_one, inv_one = factor(gram[0])
    none = jnp.zeros((M, M), F32)
    again = pair_dot((inv_one, none), gram, NN)
    again = pair_dot(again, (inv_one, none), NT)
    upper_two, inv_two = factor(again[0] + again[1])
    tri_ref[...] = exact_dot(upper_two, upper_one)
    mix = exact_dot(inv_two, inv_one)
    mix_p = -exact_dot(mix, proj, NT)

    rows = exact_dot((iota((MX, M), 0) // X == iota((MX, M), 1)).astype(F32), mix)
    for j in range(M):
        table[j] = jnp.broadcast_to(rows[:, j : j + 1], (MX, 128))
    row, col = iota((MX, KX), 0), iota((MX, KX), 1)
    n1, n2 = split2(where0(row % X == col % X, spread(mix_p, MX, KX)))
    mp[...] = jnp.concatenate([n1, n2, n1], axis=1)
    for get in gets:
        get.wait()

    def put(q):
        at = pl.ds(2 * q, 2)
        return pltpu.make_async_copy(out.at[:, at], out_hbm.at[:, at], out_sems.at[q])

    def two(q, carry):
        for i in range(2):
            f = 2 * q + i
            p1 = p_hi[f]
            both = half_dot(mp[...], jnp.concatenate([p1, p1, p_lo[f]], axis=0))
            for h in range(2):
                half = slice(h * 128, (h + 1) * 128)
                parts = [a[j, f, :, half] for j in range(M)]
                for k in range(M):
                    at = slice(k * X, (k + 1) * X)
                    total = table[0, at, :] * parts[0]
                    for j in range(1, k + 1):
                        total = total + table[j, at, :] * parts[j]
                    out[k, f, :, half] = total + both[at, half]
        put(q).start()
        return carry

    lax.fori_loop(0, TWO, two, 0)

    def end(q, carry):
        put(q).wait()
        return carry

    lax.fori_loop(0, TWO, end, 0)


def final(lines, a, p_hi, p_lo, cells):
    vmem = pl.BlockSpec(memory_space=pltpu.VMEM)
    anywhere = pl.BlockSpec(memory_space=pl.ANY)
    return pl.pallas_call(
        functools.partial(final_kernel, cells=cells),
        in_specs=[vmem, anywhere, anywhere, anywhere],
        out_specs=[anywhere, vmem, vmem],
        out_shape=[
            jax.ShapeDtypeStruct((M, F, X, Y), F32),
            jax.ShapeDtypeStruct((M, K), F32),
            jax.ShapeDtypeStruct((M, M), F32),
        ],
        scratch_shapes=[
            pltpu.VMEM((M, F, X, Y), F32),
            pltpu.VMEM((F, KX, Y), BF16),
            pltpu.VMEM((F, KX, Y), BF16),
            pltpu.VMEM((M, F, X, Y), F32),
            pltpu.VMEM((M, MX, 128), F32),
            pltpu.VMEM((MX, 3 * KX), BF16),
            pltpu.SemaphoreType.DMA((3,)),
            pltpu.SemaphoreType.DMA((TWO,)),
        ],
        name="final",
    )(lines, a, p_hi, p_lo)


def on_device(
    krylov_block, prior_basis, flux_along, flux_across, collision, field_rates, wall_table,
    wall_mask, wall_type,
):
    cells = F * X * lax.axis_size(GX) * Y * lax.axis_size(GY)
    first, last = pack(krylov_block)

    def onward(axis):
        return [(i, i + 1) for i in range(lax.axis_size(axis) - 1)]

    def back(axis):
        return [(j, i) for i, j in onward(axis)]

    before = lax.ppermute(last, GX, onward(GX))
    after = lax.ppermute(first, GX, back(GX))
    applied, yfirst, ylast, weights = inside(
        krylov_block, flux_along, flux_across, collision, wall_mask, wall_type, field_rates,
        wall_table,
    )
    ybefore = lax.ppermute(ylast, GY, onward(GY))
    yafter = lax.ppermute(yfirst, GY, back(GY))
    gp, p_hi, p_lo = basis(prior_basis)
    cb, ca = columns(ybefore, yafter, flux_across)
    sizes = [lax.axis_size(stage) for stage in STAGES]
    applied, lines = with_halo(
        applied, p_hi, p_lo, before, after, cb, ca, weights, gp, sizes[0]
    )
    lines = middle(sent_to_all(lines, STAGES[0]), sizes[1])
    lines = sent_to_all(lines, STAGES[1])
    new_block, projection, triangle = final(lines, applied, p_hi, p_lo, cells)
    return new_block, projection.T, triangle


def solution(mesh):
    torus = Mesh(mesh.devices.reshape(8, 4, 4, 2), ("gx_z", "gx_x", "gy_y", "gy_c"))
    cells = P(GX, GY)
    stack = P(None, None, GX, GY)
    in_specs = (stack, stack, P(), P(), cells, P(), P(), cells, cells)
    out_specs = (stack, P(), P())
    return jax.shard_map(
        on_device, mesh=torus, in_specs=in_specs, out_specs=out_specs, check_vma=False
    )
```

```python
import functools

import jax
import jax.numpy as jnp
from jax import lax
from jax.experimental import pallas as pl
from jax.experimental.pallas import tpu as pltpu
from jax.sharding import Mesh
from jax.sharding import PartitionSpec as P

GX = ("gx_z", "gx_x")
GY = ("gy_y", "gy_c")
STAGES = (("gx_x", "gy_y"), ("gx_z", "gy_c"))

DAMP = 0.0625
PRECISE = lax.Precision.HIGHEST
F32 = jnp.float32
BF16 = jnp.bfloat16

M = 16
K = 24
F = 26
X = 8
Y = 256
FX = F * X
MX = M * X
KX = K * X
PAIRS = M // 2
HALO = 4 * F

NN = (((1,), (0,)), ((), ()))
NT = (((1,), (1,)), ((), ()))
TN = (((0,), (0,)), ((), ()))


def exact_dot(a, b, dims=NN):
    return lax.dot_general(a, b, dims, precision=PRECISE, preferred_element_type=F32)


def half_dot(a, b, dims=NN):
    return lax.dot_general(a, b, dims, preferred_element_type=F32)


def split2(v):
    hi = v.astype(BF16)
    return hi, (v - hi.astype(F32)).astype(BF16)


def split3(v):
    hi = v.astype(BF16)
    rest = v - hi.astype(F32)
    mid = rest.astype(BF16)
    return hi, mid, (rest - mid.astype(F32)).astype(BF16)


def iota(shape, dim):
    return lax.broadcasted_iota(jnp.int32, shape, dim)


def where0(mask, v):
    return jnp.where(mask, v, jnp.zeros_like(v))


def spread(small, rows, cols):
    n, k = small.shape
    left = (iota((rows, n), 0) // X == iota((rows, n), 1)).astype(F32)
    right = (iota((k, cols), 1) // X == iota((k, cols), 0)).astype(F32)
    return exact_dot(exact_dot(left, small), right)


def two_sum(a, b):
    s = a + b
    t = s - a
    return s, (a - (s - t)) + (b - t)


def roll(v, shift, axis):
    size = v.shape[axis]
    return pltpu.roll(v, shift % size if isinstance(shift, int) else shift, axis)


def moved(v, shift):
    lane = iota((v.shape[0], 128), 1)
    left, right = roll(v[:, 0:128], shift, 1), roll(v[:, 128:], shift, 1)
    if shift > 0:
        left, right = where0(lane >= shift, left), jnp.where(lane >= shift, right, left)
    else:
        keep = lane < 128 + shift
        left, right = jnp.where(keep, left, right), where0(keep, right)
    return jnp.concatenate([left, right], axis=1)


def pack_kernel(v_hbm, first_hbm, last_hbm, v, first, last, sems):
    def get(q):
        at = pl.ds(2 * q, 2)
        return pltpu.make_async_copy(v_hbm.at[at], v.at[at], sems.at[0, q])

    def puts(q):
        return (
            pltpu.make_async_copy(first.at[q], first_hbm.at[q], sems.at[1, q]),
            pltpu.make_async_copy(last.at[q], last_hbm.at[q], sems.at[2, q]),
        )

    for q in range(PAIRS):
        get(q).start()

    def pair(q, carry):
        get(q).wait()
        for i in range(2):
            for f in range(F):
                at = (i * F + f) * 2
                first[q, at : at + 2, :] = v[2 * q + i, f, 0:2, :]
                last[q, at : at + 2, :] = v[2 * q + i, f, X - 2 : X, :]
        for put in puts(q):
            put.start()
        return carry

    lax.fori_loop(0, PAIRS, pair, 0)
    for q in range(PAIRS):
        for put in puts(q):
            put.wait()


def pack(v):
    anywhere = pl.BlockSpec(memory_space=pl.ANY)
    return pl.pallas_call(
        pack_kernel,
        in_specs=[anywhere],
        out_specs=[anywhere] * 2,
        out_shape=[jax.ShapeDtypeStruct((PAIRS, HALO, Y), F32)] * 2,
        scratch_shapes=[
            pltpu.VMEM((M, F, X, Y), F32),
            pltpu.VMEM((PAIRS, HALO, Y), F32),
            pltpu.VMEM((PAIRS, HALO, Y), F32),
            pltpu.SemaphoreType.DMA((3, PAIRS)),
        ],
        cost_estimate=pl.CostEstimate(flops=10**6, bytes_accessed=6 * 10**6, transcendentals=0),
        name="pack",
    )(v)


def inside_kernel(
    v_ref, along_ref, across_ref, coll_ref, mask_ref, type_ref, rate_ref, table_ref,
    out_ref, yfirst_ref, ylast_ref, halo_ref, ycol_ref, w, coeff, *, step_m,
):
    @pl.when(pl.program_id(0) == 0)
    def _():
        eye = (iota((F, F), 0) == iota((F, F), 1)).astype(F32)
        along, across = 0.5 * along_ref[...], 0.5 * across_ref[...]
        plus, minus = along - 4.0 * DAMP * eye, -along - 4.0 * DAMP * eye
        halves = [h for v in (plus, minus, across) for h in split2(v)]
        left = (iota((FX, F), 0) // X == iota((FX, F), 1)).astype(BF16)
        right = (iota((F, FX), 1) // X == iota((F, FX), 0)).astype(BF16)
        tall = [half_dot(left, h).astype(BF16) for h in halves]
        plus_hi, plus_lo, minus_hi, minus_lo, across_hi, across_lo = (
            half_dot(v, right) for v in tall
        )
        row, col = iota((FX, FX), 0), iota((FX, FX), 1)
        step = col % X - row % X
        far = (row // X == col // X) & (jnp.abs(step) == 2)
        hi = where0(step == 1, plus_hi) + where0(step == -1, minus_hi) + jnp.where(far, DAMP, 0.0)
        lo = where0(step == 1, plus_lo) + where0(step == -1, minus_lo)
        yhi, ylo = where0(step == 0, across_hi), where0(step == 0, across_lo)
        hi = jnp.concatenate([hi, yhi], axis=0)
        lo = jnp.concatenate([lo, ylo], axis=0)
        w[...] = jnp.concatenate([hi, lo, hi], axis=1).astype(BF16)
        ycol_ref[0] = yhi.astype(BF16)
        ycol_ref[1] = ylo.astype(BF16)
        walls = [
            jnp.where(type_ref[...] == t, mask_ref[...].astype(F32), 0.0)
            for t in range(table_ref.shape[0])
        ]
        for f in range(F):
            c = coll_ref[...] * rate_ref[f]
            for t, wall in enumerate(walls):
                c = c + wall * table_ref[t, f]
            coeff[f * X : (f + 1) * X, :] = c + 12.0 * DAMP

        row, col = iota((FX, HALO), 0), iota((FX, HALO), 1)
        x, f = row % X, row // X
        g, j, later = col % (2 * F) // 2, col % 2, col >= 2 * F
        right = (iota((F, HALO), 1) % (2 * F) // 2 == iota((F, HALO), 0)).astype(BF16)
        plus_hi, plus_lo, minus_hi, minus_lo = (half_dot(v, right) for v in tall[:4])
        edge_b = (x == 0) & (j == 1) & ~later
        edge_a = (x == X - 1) & (j == 0) & later
        outer = ((x == j) & ~later) | ((x == X - 2 + j) & later)
        hi = where0(edge_a, plus_hi) + where0(edge_b, minus_hi)
        hi = hi + jnp.where((f == g) & outer, DAMP, 0.0)
        lo = where0(edge_a, plus_lo) + where0(edge_b, minus_lo)
        halo_ref[0] = jnp.concatenate([hi, hi], axis=1).astype(BF16)
        halo_ref[1] = jnp.concatenate([lo, jnp.zeros_like(lo)], axis=1).astype(BF16)
        yfirst_ref[...] = jnp.zeros_like(yfirst_ref)
        ylast_ref[...] = jnp.zeros_like(ylast_ref)

    lane2 = iota((FX, 128), 1) // 2

    def one(i):
        m = pl.program_id(0) * step_m + i
        v = v_ref[i].reshape(FX, Y)
        mine = lane2 == m
        yfirst_ref[...] = jnp.where(mine, roll(v[:, 0:128], 2 * m, 1), yfirst_ref[...])
        ylast_ref[...] = jnp.where(mine, roll(v[:, Y - 128 :], 2 * m + 2, 1), ylast_ref[...])
        hi, lo = split2(v)
        both = half_dot(w[...], jnp.concatenate([hi, hi, lo], axis=0))
        u = both[FX:]
        out = both[:FX] + coeff[...] * v
        side = 4.0 * DAMP * v
        two = DAMP * v
        out = out + moved(u - side, -1) - moved(u + side, 1)
        out = out + moved(two, -2) + moved(two, 2)
        out_ref[i] = out.reshape(F, X, Y)

    def couple(i, carry):
        one(2 * i)
        one(2 * i + 1)
        return carry

    lax.fori_loop(0, step_m // 2, couple, 0)


def inside(v, along, across, coll, mask, types, rates, table, step_m=4):
    smem = pl.BlockSpec(memory_space=pltpu.SMEM)
    whole2 = lambda i: (0, 0)
    return pl.pallas_call(
        functools.partial(inside_kernel, step_m=step_m),
        grid=(M // step_m,),
        in_specs=[
            pl.BlockSpec((step_m, F, X, Y), lambda i: (i, 0, 0, 0)),
            pl.BlockSpec((F, F), whole2),
            pl.BlockSpec((F, F), whole2),
            pl.BlockSpec((X, Y), whole2),
            pl.BlockSpec((X, Y), whole2),
            pl.BlockSpec((X, Y), whole2),
            smem,
            smem,
        ],
        out_specs=[
            pl.BlockSpec((step_m, F, X, Y), lambda i: (i, 0, 0, 0)),
            pl.BlockSpec((FX, 128), whole2),
            pl.BlockSpec((FX, 128), whole2),
            pl.BlockSpec((2, FX, 2 * HALO), lambda i: (0, 0, 0)),
            pl.BlockSpec((2, FX, FX), lambda i: (0, 0, 0)),
        ],
        out_shape=[
            jax.ShapeDtypeStruct((M, F, X, Y), F32),
            jax.ShapeDtypeStruct((FX, 128), F32),
            jax.ShapeDtypeStruct((FX, 128), F32),
            jax.ShapeDtypeStruct((2, FX, 2 * HALO), BF16),
            jax.ShapeDtypeStruct((2, FX, FX), BF16),
        ],
        scratch_shapes=[pltpu.VMEM((2 * FX, 3 * FX), BF16), pltpu.VMEM((FX, Y), F32)],
        cost_estimate=pl.CostEstimate(
            flops=8 * 10**9, bytes_accessed=7 * 10**6, transcendentals=0
        ),
        name="inside",
    )(v, along, across, coll, mask, types, rates, table)


def diagonal(big, small, left, right):
    rows, cols = left * X, right * X
    own = iota((rows, cols), 0) % X == iota((rows, cols), 1) % X
    big = jnp.sum(where0(own, big).reshape(left, X, cols), axis=1)
    small = jnp.sum(where0(own, small).reshape(left, X, cols), axis=1)
    for shift in (4, 2, 1):
        big, err = two_sum(big, roll(big, -shift, 1))
        small = small + roll(small, -shift, 1) + err
    pick = (iota((cols, 128), 0) == X * iota((cols, 128), 1)).astype(F32)
    return exact_dot(big, pick), exact_dot(small, pick)


TWO = F // 2


def basis_kernel(p_hbm, out_ref, hi_hbm, lo_hbm, p, hi_ref, lo_ref, big_ref, small_ref, in_sem, out_sem):
    def get(f):
        return pltpu.make_async_copy(p_hbm.at[:, f], p.at[:, f], in_sem.at[f])

    def puts(q):
        at = pl.ds(TWO * q, TWO)
        return (
            pltpu.make_async_copy(hi_ref.at[at], hi_hbm.at[at], out_sem.at[0, q]),
            pltpu.make_async_copy(lo_ref.at[at], lo_hbm.at[at], out_sem.at[1, q]),
        )

    for f in range(F):
        get(f).start()
    big_ref[...] = jnp.zeros_like(big_ref)
    small_ref[...] = jnp.zeros_like(small_ref)

    def some(q, carry):
        his, los = [], []
        for i in range(TWO):
            f = q * TWO + i
            get(f).wait()
            hi, lo = split2(p[:, f].reshape(KX, Y))
            hi_ref[f] = hi
            lo_ref[f] = lo
            his.append(hi)
            los.append(lo)
        for put in puts(q):
            put.start()
        half = [lo * jnp.asarray(0.5, BF16) for lo in los]
        big_ref[...] += half_dot(jnp.concatenate(his, axis=1), jnp.concatenate(his, axis=1), NT)
        small_ref[...] += half_dot(
            jnp.concatenate(los + los, axis=1), jnp.concatenate(his + half, axis=1), NT
        )
        return carry

    lax.fori_loop(0, 2, some, 0)
    hi, lo = diagonal(big_ref[...], small_ref[...], K, K)
    eye = (iota((K, K), 0) == iota((K, 128), 1)[:, 0:K]).astype(F32)
    turned = exact_dot(lo[:, 0:K], eye, TN)
    lo = lo + jnp.concatenate([turned, jnp.zeros((K, 128 - K), F32)], axis=1)
    lane = iota((8, 128), 1)
    for half, part in enumerate((hi, lo)):
        line = where0((lane >= 80) & (lane < 104), roll(part[0:8], 80, 1))
        line = line + where0((lane >= 104) & (lane < 120), roll(part[8:16], 96, 1))
        line = line + where0(lane >= 120, roll(part[16:24], 104, 1))
        out_ref[8 * half : 8 * half + 8, :] = line

    for q in range(2):
        for put in puts(q):
            put.wait()


def basis(p):
    anywhere = pl.BlockSpec(memory_space=pl.ANY)
    return pl.pallas_call(
        basis_kernel,
        in_specs=[anywhere],
        out_specs=[pl.BlockSpec(memory_space=pltpu.VMEM), anywhere, anywhere],
        out_shape=[
            jax.ShapeDtypeStruct((16, 128), F32),
            jax.ShapeDtypeStruct((F, KX, Y), BF16),
            jax.ShapeDtypeStruct((F, KX, Y), BF16),
        ],
        scratch_shapes=[
            pltpu.VMEM((K, F, X, Y), F32),
            pltpu.VMEM((F, KX, Y), BF16),
            pltpu.VMEM((F, KX, Y), BF16),
            pltpu.VMEM((KX, KX), F32),
            pltpu.VMEM((KX, KX), F32),
            pltpu.SemaphoreType.DMA((F,)),
            pltpu.SemaphoreType.DMA((2, 2)),
        ],
        cost_estimate=pl.CostEstimate(
            flops=8 * 10**9, bytes_accessed=10 * 10**6, transcendentals=0
        ),
        name="basis",
    )(p)


def halo_kernel(
    a_hbm, hi_hbm, lo_hbm, before_hbm, after_hbm, yb_ref, ya_ref, w_ref, wy_ref, gp_ref,
    out_hbm, line_ref, a, p_hi, p_lo, before, after, edge, acc, a_sem, sems,
):
    def get(q):
        at = pl.ds(2 * q, 2)
        return (
            pltpu.make_async_copy(a_hbm.at[at], a.at[at], a_sem.at[0, q]),
            pltpu.make_async_copy(before_hbm.at[q], before.at[q], a_sem.at[1, q]),
            pltpu.make_async_copy(after_hbm.at[q], after.at[q], a_sem.at[2, q]),
        )

    def put(q):
        at = pl.ds(2 * q, 2)
        return pltpu.make_async_copy(a.at[at], out_hbm.at[at], a_sem.at[3, q])

    get_hi = pltpu.make_async_copy(hi_hbm, p_hi, sems.at[0])
    get_lo = pltpu.make_async_copy(lo_hbm, p_lo, sems.at[1])
    for q in range(PAIRS):
        for each in get(q):
            each.start()
    get_hi.start()
    get_lo.start()
    lane = iota((FX, 128), 1)
    yb, ya = yb_ref[...], ya_ref[...]
    hi, lo = split2(jnp.concatenate([yb, ya], axis=1))
    u = half_dot(wy_ref[0], hi) + half_dot(wy_ref[1], hi) + half_dot(wy_ref[0], lo)
    term = u[:, 0:128] + 4.0 * DAMP * yb
    edge[0] = DAMP * yb - where0(lane % 2 == 0, roll(term, -1, 1))
    term = u[:, 128:] - 4.0 * DAMP * ya
    edge[1] = DAMP * ya + where0(lane % 2 == 1, roll(term, 1, 1))

    def pair(q):
        for each in get(q):
            each.wait()
        for i in range(2):
            m = 2 * q + i
            mine = slice(i * 2 * F, (i + 1) * 2 * F)
            h = jnp.concatenate([before[q][mine], after[q][mine]], axis=0)
            hi = h.astype(BF16).astype(F32)
            h = jnp.concatenate([hi, h - hi], axis=0).astype(BF16)
            left = where0(lane < 2, roll(edge[0], (128 - 2 * m) % 128, 1))
            right = where0(lane >= 126, roll(edge[1], 126 - 2 * m, 1))
            part = a[m].reshape(FX, Y) + jnp.concatenate([left, right], axis=1)
            part = part + (half_dot(w_ref[0], h) + half_dot(w_ref[1], h))
            a[m] = part.reshape(F, X, Y)
        put(q).start()

    def pairs(q, carry):
        pair(2 * q)
        pair(2 * q + 1)
        return carry

    lax.fori_loop(0, PAIRS // 2, pairs, 0)
    acc[...] = jnp.zeros_like(acc)
    get_hi.wait()
    get_lo.wait()

    def some(q, carry):
        rows, cols = [], []
        for i in range(TWO):
            f = q * TWO + i
            hi, lo = split2(a[:, f].reshape(MX, Y))
            rows.append(jnp.concatenate([p_hi[f], hi, p_lo[f], lo], axis=0))
            cols.append(jnp.concatenate([hi, lo], axis=0))
        acc[...] += half_dot(jnp.concatenate(rows, axis=1), jnp.concatenate(cols, axis=1), NT)
        return carry

    lax.fori_loop(0, 2, some, 0)
    n = KX + MX
    big = acc[0:n, 0:MX]
    small = acc[0:n, MX:] + acc[n:, 0:MX] + acc[n:, MX:]
    hi, lo = diagonal(big, small, K + M, M)
    lane = iota((8, 128), 1)
    for half, part in enumerate((hi, lo)):
        line = gp_ref[8 * half : 8 * half + 8, :]
        for i in range((K + M) // 8):
            mine = (lane >= 16 * i) & (lane < 16 * i + 16)
            line = line + where0(mine, roll(part[8 * i : 8 * i + 8], 16 * i, 1))
        for copy in range(line_ref.shape[0]):
            line_ref[copy, 8 * half : 8 * half + 8, :] = line

    def end(q, carry):
        put(q).wait()
        return carry

    lax.fori_loop(0, PAIRS, end, 0)


def with_halo(a, p_hi, p_lo, before, after, yb, ya, weights, wy, gp, copies):
    vmem = pl.BlockSpec(memory_space=pltpu.VMEM)
    anywhere = pl.BlockSpec(memory_space=pl.ANY)
    return pl.pallas_call(
        halo_kernel,
        in_specs=[anywhere] * 5 + [vmem] * 5,
        out_specs=[anywhere, vmem],
        out_shape=[
            jax.ShapeDtypeStruct((M, F, X, Y), F32),
            jax.ShapeDtypeStruct((copies, 16, 128), F32),
        ],
        scratch_shapes=[
            pltpu.VMEM((M, F, X, Y), F32),
            pltpu.VMEM((F, KX, Y), BF16),
            pltpu.VMEM((F, KX, Y), BF16),
            pltpu.VMEM((PAIRS, HALO, Y), F32),
            pltpu.VMEM((PAIRS, HALO, Y), F32),
            pltpu.VMEM((2, FX, 128), F32),
            pltpu.VMEM((2 * (KX + MX), 2 * MX), F32),
            pltpu.SemaphoreType.DMA((4, PAIRS)),
            pltpu.SemaphoreType.DMA((2,)),
        ],
        cost_estimate=pl.CostEstimate(
            flops=8 * 10**9, bytes_accessed=14 * 10**6, transcendentals=0
        ),
        name="halo",
    )(a, p_hi, p_lo, before, after, yb, ya, weights, wy, gp)


def pair_total(ref):
    parts = [(ref[i, 0:8, :], ref[i, 8:16, :]) for i in range(ref.shape[0])]
    while len(parts) > 1:
        after = []
        for i in range(0, len(parts) - 1, 2):
            hi, err = two_sum(parts[i][0], parts[i + 1][0])
            after.append((hi, parts[i][1] + parts[i + 1][1] + err))
        parts = after + parts[len(parts) // 2 * 2 :]
    return parts[0]


def middle_kernel(in_ref, out_ref):
    hi, lo = pair_total(in_ref)
    hi, lo = two_sum(hi, lo)
    for i in range(out_ref.shape[0]):
        out_ref[i, 0:8, :] = hi
        out_ref[i, 8:16, :] = lo


def middle(lines, copies):
    return pl.pallas_call(
        middle_kernel,
        out_shape=jax.ShapeDtypeStruct((copies, 16, 128), F32),
        name="middle",
    )(lines)


def sent_to_all(copies, axis):
    return lax.all_to_all(copies, axis, split_axis=0, concat_axis=0, tiled=True)


def grid_of(v, top):
    return (v + top) - top


def slices(hi, lo, axis):
    top = jnp.max(jnp.abs(hi), axis=axis, keepdims=True)
    first = grid_of(hi, top * 2.0**16)
    rest = hi - first
    second = grid_of(rest, top * 2.0**8)
    return first, second, (rest - second) + lo


def pair_dot(a, b, dims):
    a1, a2, a3 = slices(*a, dims[0][0][0])
    b1, b2, b3 = slices(*b, dims[0][1][0])
    dot = functools.partial(exact_dot, dims=dims)
    h1, h2, k1, k2 = (v.astype(BF16) for v in (a1, a2, b1, b2))
    big = half_dot(h1, k1, dims)
    mid = half_dot(h1, k2, dims) + half_dot(h2, k1, dims)
    low = dot(a1, b3) + dot(a2, b2 + b3) + dot(a3, b1 + b2)
    big, err = two_sum(big, mid)
    return two_sum(big, err + low)


def pair_add(a, b):
    big, err = two_sum(a[0], b[0])
    return two_sum(big, err + (a[1] + b[1]))


def factor(gram):
    n = gram.shape[0]
    row, lane = iota((n, 128), 0), iota((n, 128), 1)
    eye = (iota((n, n), 0) == iota((n, n), 1)).astype(F32)
    t = jnp.concatenate([gram, eye, jnp.zeros((n, 128 - 2 * n), F32)], axis=1)
    columns = [jnp.broadcast_to(gram[:, k : k + 1], (n, 128)) for k in range(n)]
    pivots = jnp.zeros((n, 128), F32)

    def line(v, k):
        return jnp.broadcast_to(v[k : k + 1, :], (n, 128))

    for k in range(n):
        pivot = line(columns[k], k)
        pivots = jnp.where(row == k, pivot, pivots)
        if k == n - 1:
            break
        times = where0(row > k, columns[k]) * (1.0 / pivot)
        for j in range(k + 1, n):
            columns[j] = columns[j] - times * line(columns[k], j)
        t = t - times * line(t, k)
    t = t / jnp.sqrt(pivots)
    upper = where0(row <= lane, t)[:, 0:n]
    return upper, t[:, n : 2 * n]


def final_kernel(
    line_ref, a_hbm, hi_hbm, lo_hbm, out_hbm, proj_ref, tri_ref,
    a, p_hi, p_lo, out, table, mp, both, in_sems, out_sems, *, cells,
):
    gets = [
        pltpu.make_async_copy(src, dst, in_sems.at[i])
        for i, (src, dst) in enumerate(((a_hbm, a), (hi_hbm, p_hi), (lo_hbm, p_lo)))
    ]
    for get in gets:
        get.start()

    hi, lo = pair_total(line_ref)
    hi, lo = two_sum(hi, lo)
    odd = cells
    while odd % 2 == 0:
        odd //= 2
    scale = float(odd) / float(cells)
    guess = hi / float(odd)
    big = guess * 4097.0
    big = big - (big - guess)
    left = ((hi - big * float(odd)) - (guess - big) * float(odd)) + lo
    hi, lo = two_sum(guess, left / float(odd))
    hi, lo = hi * scale, lo * scale

    lane8 = iota((8, 128), 1)

    def unpack(v):
        rows = [roll(v, -16 * i, 1) for i in range(5)]
        top = where0(lane8 < 24, roll(v, -80, 1))
        centre = where0((lane8 >= 8) & (lane8 < 24), roll(v, -96, 1))
        end = where0((lane8 >= 16) & (lane8 < 24), roll(v, -104, 1))
        upper = jnp.concatenate([top, centre, end], axis=0)[:, 0:K]
        off = where0(iota((K, K), 1) // 8 > iota((K, K), 0) // 8, upper)
        eye = (iota((K, K), 0) == iota((K, K), 1)).astype(F32)
        return (
            jnp.concatenate(rows[0:3], axis=0)[:, 0:M],
            jnp.concatenate(rows[3:5], axis=0)[:, 0:M],
            upper + exact_dot(eye, off, NT),
        )

    (c_hi, s_hi, g_hi), (c_lo, s_lo, g_lo) = unpack(hi), unpack(lo)
    zero = jnp.zeros((K, M), F32)
    second = c_hi - exact_dot(g_hi, c_hi)
    proj = c_hi + second
    eye = (iota((K, K), 0) == iota((K, K), 1)).astype(F32)
    proj_ref[...] = exact_dot(proj, eye, TN)
    gp = pair_dot((g_hi, g_lo), (proj, zero), NN)
    t_hi, t_lo = pair_add(gp, (-c_hi, -c_lo))
    gram = pair_dot(
        (jnp.concatenate([proj, c_hi], axis=0), jnp.concatenate([zero, c_lo], axis=0)),
        (jnp.concatenate([t_hi, -proj], axis=0), jnp.concatenate([t_lo, zero], axis=0)),
        TN,
    )
    gram = pair_add((s_hi, s_lo), gram)
    upper_one, inv_one = factor(gram[0])
    none = jnp.zeros((M, M), F32)
    again = pair_dot((inv_one, none), gram, NN)
    again = pair_dot(again, (inv_one, none), NT)
    right = (iota((K, KX), 1) // X == iota((K, KX), 0)).astype(F32)
    wide = exact_dot(exact_dot(inv_one, proj, NT), right)
    wide = jnp.concatenate([wide, inv_one], axis=1)
    upper_two, inv_two = factor(again[0] + again[1])
    tri_ref[...] = exact_dot(upper_two, upper_one)
    left = (iota((MX, M), 0) // X == iota((MX, M), 1)).astype(F32)
    wide = exact_dot(exact_dot(left, inv_two), wide)
    rows = wide[:, KX:]
    for j in range(M):
        table[j] = jnp.broadcast_to(rows[:, j : j + 1], (MX, 128))
    row, col = iota((MX, KX), 0), iota((MX, KX), 1)
    n1, n2 = split2(where0(row % X == col % X, -wide[:, 0:KX]))
    mp[...] = jnp.concatenate([n1, n2, n1], axis=1)
    for get in gets:
        get.wait()

    def put(f):
        return pltpu.make_async_copy(out.at[:, f], out_hbm.at[:, f], out_sems.at[f])

    def basis_part(f):
        p1 = p_hi[f]
        return half_dot(mp[...], jnp.concatenate([p1, p1, p_lo[f]], axis=0))

    def one(f, slot):
        both[1 - slot] = basis_part(jnp.minimum(f + 1, F - 1))

        halves = [slice(h * 128, (h + 1) * 128) for h in range(2)]
        parts = [[a[j, f, :, half] for half in halves] for j in range(M)]
        for k in range(M):
            at = slice(k * X, (k + 1) * X)
            totals = [both[slot, at, half] for half in halves]
            for j in range(k + 1):
                times = table[j, at, :]
                totals = [total + times * part for total, part in zip(totals, parts[j])]
            for half, total in zip(halves, totals):
                out[k, f, :, half] = total
        put(f).start()

    both[0] = basis_part(0)

    def two(q, carry):
        one(2 * q, 0)
        one(2 * q + 1, 1)
        return carry

    lax.fori_loop(0, TWO, two, 0)

    def end(f, carry):
        put(f).wait()
        return carry

    lax.fori_loop(0, F, end, 0)


def final(lines, a, p_hi, p_lo, cells):
    vmem = pl.BlockSpec(memory_space=pltpu.VMEM)
    anywhere = pl.BlockSpec(memory_space=pl.ANY)
    return pl.pallas_call(
        functools.partial(final_kernel, cells=cells),
        in_specs=[vmem, anywhere, anywhere, anywhere],
        out_specs=[anywhere, vmem, vmem],
        out_shape=[
            jax.ShapeDtypeStruct((M, F, X, Y), F32),
            jax.ShapeDtypeStruct((M, K), F32),
            jax.ShapeDtypeStruct((M, M), F32),
        ],
        scratch_shapes=[
            pltpu.VMEM((M, F, X, Y), F32),
            pltpu.VMEM((F, KX, Y), BF16),
            pltpu.VMEM((F, KX, Y), BF16),
            pltpu.VMEM((M, F, X, Y), F32),
            pltpu.VMEM((M, MX, 128), F32),
            pltpu.VMEM((MX, 3 * KX), BF16),
            pltpu.VMEM((2, MX, Y), F32),
            pltpu.SemaphoreType.DMA((3,)),
            pltpu.SemaphoreType.DMA((F,)),
        ],
        name="final",
    )(lines, a, p_hi, p_lo)


def on_device(
    krylov_block, prior_basis, flux_along, flux_across, collision, field_rates, wall_table,
    wall_mask, wall_type,
):
    cells = F * X * lax.axis_size(GX) * Y * lax.axis_size(GY)
    first, last = pack(krylov_block)

    def onward(axis):
        return [(i, i + 1) for i in range(lax.axis_size(axis) - 1)]

    def back(axis):
        return [(j, i) for i, j in onward(axis)]

    before = lax.ppermute(last, GX, onward(GX))
    after = lax.ppermute(first, GX, back(GX))
    applied, yfirst, ylast, weights, wy = inside(
        krylov_block, flux_along, flux_across, collision, wall_mask, wall_type, field_rates,
        wall_table,
    )
    ybefore = lax.ppermute(ylast, GY, onward(GY))
    yafter = lax.ppermute(yfirst, GY, back(GY))
    gp, p_hi, p_lo = basis(prior_basis)
    sizes = [lax.axis_size(stage) for stage in STAGES]
    applied, lines = with_halo(
        applied, p_hi, p_lo, before, after, ybefore, yafter, weights, wy, gp, sizes[0]
    )
    lines = middle(sent_to_all(lines, STAGES[0]), sizes[1])
    lines = sent_to_all(lines, STAGES[1])
    new_block, projection, triangle = final(lines, applied, p_hi, p_lo, cells)
    return new_block, projection.T, triangle


def solution(mesh):
    torus = Mesh(mesh.devices.reshape(8, 4, 4, 2), ("gx_z", "gx_x", "gy_y", "gy_c"))
    cells = P(GX, GY)
    stack = P(None, None, GX, GY)
    in_specs = (stack, stack, P(), P(), cells, P(), P(), cells, cells)
    out_specs = (stack, P(), P())
    return jax.shard_map(
        on_device, mesh=torus, in_specs=in_specs, out_specs=out_specs, check_vma=False
    )
```

```python
import functools

import jax
import jax.numpy as jnp
from jax import lax
from jax.experimental import pallas as pl
from jax.experimental.pallas import tpu as pltpu
from jax.sharding import Mesh
from jax.sharding import PartitionSpec as P

GX = ("gx_z", "gx_x")
GY = ("gy_y", "gy_c")
STAGES = (("gx_x", "gy_y"), ("gx_z", "gy_c"))

DAMP = 0.0625
PRECISE = lax.Precision.HIGHEST
F32 = jnp.float32
BF16 = jnp.bfloat16

M = 16
K = 24
F = 26
X = 8
Y = 256
FX = F * X
MX = M * X
KX = K * X
PAIRS = M // 2
LIMIT = 32 * 2**20
HALO = 4 * F

NN = (((1,), (0,)), ((), ()))
NT = (((1,), (1,)), ((), ()))
TN = (((0,), (0,)), ((), ()))


def exact_dot(a, b, dims=NN):
    return lax.dot_general(a, b, dims, precision=PRECISE, preferred_element_type=F32)


def half_dot(a, b, dims=NN):
    return lax.dot_general(a, b, dims, preferred_element_type=F32)


def split2(v):
    hi = v.astype(BF16)
    return hi, (v - hi.astype(F32)).astype(BF16)


def split3(v):
    hi = v.astype(BF16)
    rest = v - hi.astype(F32)
    mid = rest.astype(BF16)
    return hi, mid, (rest - mid.astype(F32)).astype(BF16)


def kept(*shape_and_type):
    return pltpu.VMEM(*shape_and_type)


def near(v):
    return pltpu.with_memory_space_constraint(v, pltpu.VMEM)


def iota(shape, dim):
    return lax.broadcasted_iota(jnp.int32, shape, dim)


def where0(mask, v):
    return jnp.where(mask, v, jnp.zeros_like(v))


def spread(small, rows, cols):
    n, k = small.shape
    left = (iota((rows, n), 0) // X == iota((rows, n), 1)).astype(F32)
    right = (iota((k, cols), 1) // X == iota((k, cols), 0)).astype(F32)
    return exact_dot(exact_dot(left, small), right)


def two_sum(a, b):
    s = a + b
    t = s - a
    return s, (a - (s - t)) + (b - t)


def roll(v, shift, axis):
    size = v.shape[axis]
    return pltpu.roll(v, shift % size if isinstance(shift, int) else shift, axis)


def moved(v, shift):
    lane = iota((v.shape[0], 128), 1)
    left, right = roll(v[:, 0:128], shift, 1), roll(v[:, 128:], shift, 1)
    if shift > 0:
        left, right = where0(lane >= shift, left), jnp.where(lane >= shift, right, left)
    else:
        keep = lane < 128 + shift
        left, right = jnp.where(keep, left, right), where0(keep, right)
    return jnp.concatenate([left, right], axis=1)


def pack_kernel(v, first, last):
    def pair(q, carry):
        for i in range(2):
            for f in range(F):
                at = (i * F + f) * 2
                first[q, at : at + 2, :] = v[2 * q + i, f, 0:2, :]
                last[q, at : at + 2, :] = v[2 * q + i, f, X - 2 : X, :]
        return carry

    lax.fori_loop(0, PAIRS, pair, 0)


def pack(v):
    vmem = pl.BlockSpec(memory_space=pltpu.VMEM)
    return pl.pallas_call(
        pack_kernel,
        in_specs=[vmem],
        out_specs=[vmem] * 2,
        out_shape=[kept((PAIRS, HALO, Y), F32)] * 2,
        compiler_params=pltpu.CompilerParams(vmem_limit_bytes=LIMIT),
        cost_estimate=pl.CostEstimate(flops=10**6, bytes_accessed=6 * 10**6, transcendentals=0),
        name="pack",
    )(near(v))


def inside_kernel(
    v_ref, along_ref, across_ref, coll_ref, mask_ref, type_ref, rate_ref, table_ref,
    out_ref, yfirst_ref, ylast_ref, halo_ref, ycol_ref, w, coeff, both,
):
    if True:
        eye = (iota((F, F), 0) == iota((F, F), 1)).astype(F32)
        along, across = 0.5 * along_ref[...], 0.5 * across_ref[...]
        plus, minus = along - 4.0 * DAMP * eye, -along - 4.0 * DAMP * eye
        halves = [h for v in (plus, minus, across) for h in split2(v)]
        left = (iota((FX, F), 0) // X == iota((FX, F), 1)).astype(BF16)
        right = (iota((F, FX), 1) // X == iota((F, FX), 0)).astype(BF16)
        tall = [half_dot(left, h).astype(BF16) for h in halves]
        plus_hi, plus_lo, minus_hi, minus_lo, across_hi, across_lo = (
            half_dot(v, right) for v in tall
        )
        row, col = iota((FX, FX), 0), iota((FX, FX), 1)
        step = col % X - row % X
        far = (row // X == col // X) & (jnp.abs(step) == 2)
        hi = where0(step == 1, plus_hi) + where0(step == -1, minus_hi) + jnp.where(far, DAMP, 0.0)
        lo = where0(step == 1, plus_lo) + where0(step == -1, minus_lo)
        yhi, ylo = where0(step == 0, across_hi), where0(step == 0, across_lo)
        hi = jnp.concatenate([hi, yhi], axis=0)
        lo = jnp.concatenate([lo, ylo], axis=0)
        w[...] = jnp.concatenate([hi, lo, hi], axis=1).astype(BF16)
        ycol_ref[0] = yhi.astype(BF16)
        ycol_ref[1] = ylo.astype(BF16)
        walls = [
            jnp.where(type_ref[...] == t, mask_ref[...].astype(F32), 0.0)
            for t in range(table_ref.shape[0])
        ]
        for f in range(F):
            c = coll_ref[...] * rate_ref[f]
            for t, wall in enumerate(walls):
                c = c + wall * table_ref[t, f]
            coeff[f * X : (f + 1) * X, :] = c + 12.0 * DAMP

        row, col = iota((FX, HALO), 0), iota((FX, HALO), 1)
        x, f = row % X, row // X
        g, j, later = col % (2 * F) // 2, col % 2, col >= 2 * F
        right = (iota((F, HALO), 1) % (2 * F) // 2 == iota((F, HALO), 0)).astype(BF16)
        plus_hi, plus_lo, minus_hi, minus_lo = (half_dot(v, right) for v in tall[:4])
        edge_b = (x == 0) & (j == 1) & ~later
        edge_a = (x == X - 1) & (j == 0) & later
        outer = ((x == j) & ~later) | ((x == X - 2 + j) & later)
        hi = where0(edge_a, plus_hi) + where0(edge_b, minus_hi)
        hi = hi + jnp.where((f == g) & outer, DAMP, 0.0)
        lo = where0(edge_a, plus_lo) + where0(edge_b, minus_lo)
        halo_ref[0] = jnp.concatenate([hi, hi], axis=1).astype(BF16)
        halo_ref[1] = jnp.concatenate([lo, jnp.zeros_like(lo)], axis=1).astype(BF16)
        yfirst_ref[...] = jnp.zeros_like(yfirst_ref)
        ylast_ref[...] = jnp.zeros_like(ylast_ref)

    lane2 = iota((FX, 128), 1) // 2

    def product(m):
        hi, lo = split2(v_ref[m].reshape(FX, Y))
        return half_dot(w[...], jnp.concatenate([hi, hi, lo], axis=0))

    def one(m, slot):
        both[1 - slot] = product(jnp.minimum(m + 1, M - 1))
        v = v_ref[m].reshape(FX, Y)
        mine = lane2 == m
        yfirst_ref[...] = jnp.where(mine, roll(v[:, 0:128], 2 * m, 1), yfirst_ref[...])
        ylast_ref[...] = jnp.where(mine, roll(v[:, Y - 128 :], 2 * m + 2, 1), ylast_ref[...])
        u = both[slot, FX:]
        out = both[slot, :FX] + coeff[...] * v
        side = 4.0 * DAMP * v
        two = DAMP * v
        out = out + moved(u - side, -1) - moved(u + side, 1)
        out = out + moved(two, -2) + moved(two, 2)
        out_ref[m] = out.reshape(F, X, Y)

    both[0] = product(0)

    def couple(i, carry):
        one(2 * i, 0)
        one(2 * i + 1, 1)
        return carry

    lax.fori_loop(0, M // 2, couple, 0)


def inside(v, along, across, coll, mask, types, rates, table):
    smem = pl.BlockSpec(memory_space=pltpu.SMEM)
    vmem = pl.BlockSpec(memory_space=pltpu.VMEM)
    return pl.pallas_call(
        inside_kernel,
        in_specs=[vmem] * 6 + [smem] * 2,
        out_specs=[vmem] * 5,
        out_shape=[
            kept((M, F, X, Y), F32),
            kept((FX, 128), F32),
            kept((FX, 128), F32),
            kept((2, FX, 2 * HALO), BF16),
            kept((2, FX, FX), BF16),
        ],
        scratch_shapes=[
            pltpu.VMEM((2 * FX, 3 * FX), BF16),
            pltpu.VMEM((FX, Y), F32),
            pltpu.VMEM((2, 2 * FX, Y), F32),
        ],
        compiler_params=pltpu.CompilerParams(vmem_limit_bytes=LIMIT),
        cost_estimate=pl.CostEstimate(
            flops=8 * 10**9, bytes_accessed=7 * 10**6, transcendentals=0
        ),
        name="inside",
    )(near(v), along, across, coll, mask, types, rates, table)


def diagonal(big, small, left, right):
    rows, cols = left * X, right * X
    own = iota((rows, cols), 0) % X == iota((rows, cols), 1) % X
    big = jnp.sum(where0(own, big).reshape(left, X, cols), axis=1)
    small = jnp.sum(where0(own, small).reshape(left, X, cols), axis=1)
    for shift in (4, 2, 1):
        big, err = two_sum(big, roll(big, -shift, 1))
        small = small + roll(small, -shift, 1) + err
    pick = (iota((cols, 128), 0) == X * iota((cols, 128), 1)).astype(F32)
    return exact_dot(big, pick), exact_dot(small, pick)


TWO = F // 2


def basis_kernel(p, out_ref, hi_ref, lo_ref, big_ref, small_ref):
    big_ref[...] = jnp.zeros_like(big_ref)
    small_ref[...] = jnp.zeros_like(small_ref)

    def some(q, carry):
        his, los = [], []
        for i in range(TWO):
            f = q * TWO + i
            hi, lo = split2(p[:, f].reshape(KX, Y))
            hi_ref[f] = hi
            lo_ref[f] = lo
            his.append(hi)
            los.append(lo)
        half = [lo * jnp.asarray(0.5, BF16) for lo in los]
        big_ref[...] += half_dot(jnp.concatenate(his, axis=1), jnp.concatenate(his, axis=1), NT)
        small_ref[...] += half_dot(
            jnp.concatenate(los + los, axis=1), jnp.concatenate(his + half, axis=1), NT
        )
        return carry

    lax.fori_loop(0, 2, some, 0)
    hi, lo = diagonal(big_ref[...], small_ref[...], K, K)
    eye = (iota((K, K), 0) == iota((K, 128), 1)[:, 0:K]).astype(F32)
    turned = exact_dot(lo[:, 0:K], eye, TN)
    lo = lo + jnp.concatenate([turned, jnp.zeros((K, 128 - K), F32)], axis=1)
    lane = iota((8, 128), 1)
    for half, part in enumerate((hi, lo)):
        line = where0((lane >= 80) & (lane < 104), roll(part[0:8], 80, 1))
        line = line + where0((lane >= 104) & (lane < 120), roll(part[8:16], 96, 1))
        line = line + where0(lane >= 120, roll(part[16:24], 104, 1))
        out_ref[8 * half : 8 * half + 8, :] = line


def basis(p):
    vmem = pl.BlockSpec(memory_space=pltpu.VMEM)
    return pl.pallas_call(
        basis_kernel,
        in_specs=[vmem],
        out_specs=[vmem] * 3,
        out_shape=[kept((16, 128), F32), kept((F, KX, Y), BF16), kept((F, KX, Y), BF16)],
        scratch_shapes=[pltpu.VMEM((KX, KX), F32), pltpu.VMEM((KX, KX), F32)],
        compiler_params=pltpu.CompilerParams(vmem_limit_bytes=LIMIT),
        cost_estimate=pl.CostEstimate(
            flops=8 * 10**9, bytes_accessed=10 * 10**6, transcendentals=0
        ),
        name="basis",
    )(near(p))


def halo_kernel(
    inner, p_hi, p_lo, before, after, yb_ref, ya_ref, w_ref, wy_ref, gp_ref,
    a, line_ref, edge, acc,
):
    lane = iota((FX, 128), 1)
    yb, ya = yb_ref[...], ya_ref[...]
    hi, lo = split2(jnp.concatenate([yb, ya], axis=1))
    u = half_dot(wy_ref[0], hi) + half_dot(wy_ref[1], hi) + half_dot(wy_ref[0], lo)
    term = u[:, 0:128] + 4.0 * DAMP * yb
    edge[0] = DAMP * yb - where0(lane % 2 == 0, roll(term, -1, 1))
    term = u[:, 128:] - 4.0 * DAMP * ya
    edge[1] = DAMP * ya + where0(lane % 2 == 1, roll(term, 1, 1))

    def pair(q):
        for i in range(2):
            m = 2 * q + i
            mine = slice(i * 2 * F, (i + 1) * 2 * F)
            h = jnp.concatenate([before[q][mine], after[q][mine]], axis=0)
            hi = h.astype(BF16).astype(F32)
            h = jnp.concatenate([hi, h - hi], axis=0).astype(BF16)
            left = where0(lane < 2, roll(edge[0], (128 - 2 * m) % 128, 1))
            right = where0(lane >= 126, roll(edge[1], 126 - 2 * m, 1))
            part = inner[m].reshape(FX, Y) + jnp.concatenate([left, right], axis=1)
            part = part + (half_dot(w_ref[0], h) + half_dot(w_ref[1], h))
            a[m] = part.reshape(F, X, Y)

    def pairs(q, carry):
        pair(2 * q)
        pair(2 * q + 1)
        return carry

    lax.fori_loop(0, PAIRS // 2, pairs, 0)
    acc[...] = jnp.zeros_like(acc)
    def some(q, carry):
        rows, cols = [], []
        for i in range(TWO):
            f = q * TWO + i
            hi, lo = split2(a[:, f].reshape(MX, Y))
            rows.append(jnp.concatenate([p_hi[f], hi, p_lo[f], lo], axis=0))
            cols.append(jnp.concatenate([hi, lo], axis=0))
        acc[...] += half_dot(jnp.concatenate(rows, axis=1), jnp.concatenate(cols, axis=1), NT)
        return carry

    lax.fori_loop(0, 2, some, 0)
    n = KX + MX
    big = acc[0:n, 0:MX]
    small = acc[0:n, MX:] + acc[n:, 0:MX] + acc[n:, MX:]
    hi, lo = diagonal(big, small, K + M, M)
    lane = iota((8, 128), 1)
    for half, part in enumerate((hi, lo)):
        line = gp_ref[8 * half : 8 * half + 8, :]
        for i in range((K + M) // 8):
            mine = (lane >= 16 * i) & (lane < 16 * i + 16)
            line = line + where0(mine, roll(part[8 * i : 8 * i + 8], 16 * i, 1))
        for copy in range(line_ref.shape[0]):
            line_ref[copy, 8 * half : 8 * half + 8, :] = line


def with_halo(a, p_hi, p_lo, before, after, yb, ya, weights, wy, gp, copies):
    vmem = pl.BlockSpec(memory_space=pltpu.VMEM)
    return pl.pallas_call(
        halo_kernel,
        in_specs=[vmem] * 10,
        out_specs=[vmem, vmem],
        out_shape=[kept((M, F, X, Y), F32), kept((copies, 16, 128), F32)],
        scratch_shapes=[
            pltpu.VMEM((2, FX, 128), F32),
            pltpu.VMEM((2 * (KX + MX), 2 * MX), F32),
        ],
        input_output_aliases={0: 0},
        compiler_params=pltpu.CompilerParams(vmem_limit_bytes=LIMIT),
        cost_estimate=pl.CostEstimate(
            flops=8 * 10**9, bytes_accessed=14 * 10**6, transcendentals=0
        ),
        name="halo",
    )(
        near(a), near(p_hi), near(p_lo), near(before), near(after), near(yb), near(ya), weights,
        wy, gp,
    )


def pair_total(ref):
    parts = [(ref[i, 0:8, :], ref[i, 8:16, :]) for i in range(ref.shape[0])]
    while len(parts) > 1:
        after = []
        for i in range(0, len(parts) - 1, 2):
            hi, err = two_sum(parts[i][0], parts[i + 1][0])
            after.append((hi, parts[i][1] + parts[i + 1][1] + err))
        parts = after + parts[len(parts) // 2 * 2 :]
    return parts[0]


def middle_kernel(in_ref, out_ref):
    hi, lo = pair_total(in_ref)
    hi, lo = two_sum(hi, lo)
    for i in range(out_ref.shape[0]):
        out_ref[i, 0:8, :] = hi
        out_ref[i, 8:16, :] = lo


def middle(lines, copies):
    return pl.pallas_call(
        middle_kernel,
        out_shape=kept((copies, 16, 128), F32),
        compiler_params=pltpu.CompilerParams(vmem_limit_bytes=LIMIT),
        name="middle",
    )(near(lines))


def sent_to_all(copies, axis):
    return lax.all_to_all(copies, axis, split_axis=0, concat_axis=0, tiled=True)


def grid_of(v, top):
    return (v + top) - top


def slices(hi, lo, axis):
    top = jnp.max(jnp.abs(hi), axis=axis, keepdims=True)
    first = grid_of(hi, top * 2.0**16)
    rest = hi - first
    second = grid_of(rest, top * 2.0**8)
    return first, second, (rest - second) + lo


def pair_dot(a, b, dims):
    a1, a2, a3 = slices(*a, dims[0][0][0])
    b1, b2, b3 = slices(*b, dims[0][1][0])
    dot = functools.partial(exact_dot, dims=dims)
    h1, h2, k1, k2 = (v.astype(BF16) for v in (a1, a2, b1, b2))
    big = half_dot(h1, k1, dims)
    mid = half_dot(h1, k2, dims) + half_dot(h2, k1, dims)
    low = dot(a1, b3) + dot(a2, b2 + b3) + dot(a3, b1 + b2)
    big, err = two_sum(big, mid)
    return two_sum(big, err + low)


def pair_add(a, b):
    big, err = two_sum(a[0], b[0])
    return two_sum(big, err + (a[1] + b[1]))


def factor(gram):
    n = gram.shape[0]
    row, lane = iota((n, 128), 0), iota((n, 128), 1)
    eye = (iota((n, n), 0) == iota((n, n), 1)).astype(F32)
    t = jnp.concatenate([gram, eye, jnp.zeros((n, 128 - 2 * n), F32)], axis=1)
    columns = [jnp.broadcast_to(gram[:, k : k + 1], (n, 128)) for k in range(n)]
    pivots = jnp.zeros((n, 128), F32)

    def line(v, k):
        return jnp.broadcast_to(v[k : k + 1, :], (n, 128))

    for k in range(n):
        pivot = line(columns[k], k)
        pivots = jnp.where(row == k, pivot, pivots)
        if k == n - 1:
            break
        times = where0(row > k, columns[k]) * (1.0 / pivot)
        for j in range(k + 1, n):
            columns[j] = columns[j] - times * line(columns[k], j)
        t = t - times * line(t, k)
    t = t / jnp.sqrt(pivots)
    upper = where0(row <= lane, t)[:, 0:n]
    return upper, t[:, n : 2 * n]


def final_kernel(
    line_ref, a, p_hi, p_lo, out_hbm, proj_ref, tri_ref,
    out, table, mp, both, out_sems, *, cells,
):
    hi, lo = pair_total(line_ref)
    hi, lo = two_sum(hi, lo)
    odd = cells
    while odd % 2 == 0:
        odd //= 2
    scale = float(odd) / float(cells)
    guess = hi / float(odd)
    big = guess * 4097.0
    big = big - (big - guess)
    left = ((hi - big * float(odd)) - (guess - big) * float(odd)) + lo
    hi, lo = two_sum(guess, left / float(odd))
    hi, lo = hi * scale, lo * scale

    lane8 = iota((8, 128), 1)

    def unpack(v):
        rows = [roll(v, -16 * i, 1) for i in range(5)]
        top = where0(lane8 < 24, roll(v, -80, 1))
        centre = where0((lane8 >= 8) & (lane8 < 24), roll(v, -96, 1))
        end = where0((lane8 >= 16) & (lane8 < 24), roll(v, -104, 1))
        upper = jnp.concatenate([top, centre, end], axis=0)[:, 0:K]
        off = where0(iota((K, K), 1) // 8 > iota((K, K), 0) // 8, upper)
        eye = (iota((K, K), 0) == iota((K, K), 1)).astype(F32)
        return (
            jnp.concatenate(rows[0:3], axis=0)[:, 0:M],
            jnp.concatenate(rows[3:5], axis=0)[:, 0:M],
            upper + exact_dot(eye, off, NT),
        )

    (c_hi, s_hi, g_hi), (c_lo, s_lo, g_lo) = unpack(hi), unpack(lo)
    zero = jnp.zeros((K, M), F32)
    second = c_hi - exact_dot(g_hi, c_hi)
    proj = c_hi + second
    eye = (iota((K, K), 0) == iota((K, K), 1)).astype(F32)
    proj_ref[...] = exact_dot(proj, eye, TN)
    gp = pair_dot((g_hi, g_lo), (proj, zero), NN)
    t_hi, t_lo = pair_add(gp, (-c_hi, -c_lo))
    gram = pair_dot(
        (jnp.concatenate([proj, c_hi], axis=0), jnp.concatenate([zero, c_lo], axis=0)),
        (jnp.concatenate([t_hi, -proj], axis=0), jnp.concatenate([t_lo, zero], axis=0)),
        TN,
    )
    gram = pair_add((s_hi, s_lo), gram)
    upper_one, inv_one = factor(gram[0])
    none = jnp.zeros((M, M), F32)
    again = pair_dot((inv_one, none), gram, NN)
    again = pair_dot(again, (inv_one, none), NT)
    right = (iota((K, KX), 1) // X == iota((K, KX), 0)).astype(F32)
    wide = exact_dot(exact_dot(inv_one, proj, NT), right)
    wide = jnp.concatenate([wide, inv_one], axis=1)
    upper_two, inv_two = factor(again[0] + again[1])
    tri_ref[...] = exact_dot(upper_two, upper_one)
    left = (iota((MX, M), 0) // X == iota((MX, M), 1)).astype(F32)
    wide = exact_dot(exact_dot(left, inv_two), wide)
    rows = wide[:, KX:]
    for j in range(M):
        table[j] = jnp.broadcast_to(rows[:, j : j + 1], (MX, 128))
    row, col = iota((MX, KX), 0), iota((MX, KX), 1)
    n1, n2 = split2(where0(row % X == col % X, -wide[:, 0:KX]))
    mp[...] = jnp.concatenate([n1, n2, n1], axis=1)
    def put(f):
        return pltpu.make_async_copy(out.at[:, f], out_hbm.at[:, f], out_sems.at[f])

    def basis_part(f):
        p1 = p_hi[f]
        return half_dot(mp[...], jnp.concatenate([p1, p1, p_lo[f]], axis=0))

    def one(f, slot):
        both[1 - slot] = basis_part(jnp.minimum(f + 1, F - 1))

        halves = [slice(h * 128, (h + 1) * 128) for h in range(2)]
        parts = [[a[j, f, :, half] for half in halves] for j in range(M)]
        for k in range(M):
            at = slice(k * X, (k + 1) * X)
            totals = [both[slot, at, half] for half in halves]
            for j in range(k + 1):
                times = table[j, at, :]
                totals = [total + times * part for total, part in zip(totals, parts[j])]
            for half, total in zip(halves, totals):
                out[k, f, :, half] = total
        put(f).start()

    both[0] = basis_part(0)

    def two(q, carry):
        one(2 * q, 0)
        one(2 * q + 1, 1)
        return carry

    lax.fori_loop(0, TWO, two, 0)

    def end(f, carry):
        put(f).wait()
        return carry

    lax.fori_loop(0, F, end, 0)


def final(lines, a, p_hi, p_lo, cells):
    vmem = pl.BlockSpec(memory_space=pltpu.VMEM)
    anywhere = pl.BlockSpec(memory_space=pl.ANY)
    return pl.pallas_call(
        functools.partial(final_kernel, cells=cells),
        in_specs=[vmem] * 4,
        out_specs=[anywhere, vmem, vmem],
        out_shape=[
            jax.ShapeDtypeStruct((M, F, X, Y), F32),
            jax.ShapeDtypeStruct((M, K), F32),
            jax.ShapeDtypeStruct((M, M), F32),
        ],
        scratch_shapes=[
            pltpu.VMEM((M, F, X, Y), F32),
            pltpu.VMEM((M, MX, 128), F32),
            pltpu.VMEM((MX, 3 * KX), BF16),
            pltpu.VMEM((2, MX, Y), F32),
            pltpu.SemaphoreType.DMA((F,)),
        ],
        compiler_params=pltpu.CompilerParams(vmem_limit_bytes=LIMIT),
        name="final",
    )(near(lines), near(a), near(p_hi), near(p_lo))


def on_device(
    krylov_block, prior_basis, flux_along, flux_across, collision, field_rates, wall_table,
    wall_mask, wall_type,
):
    cells = F * X * lax.axis_size(GX) * Y * lax.axis_size(GY)
    first, last = pack(krylov_block)

    def onward(axis):
        return [(i, i + 1) for i in range(lax.axis_size(axis) - 1)]

    def back(axis):
        return [(j, i) for i, j in onward(axis)]

    before = lax.ppermute(last, GX, onward(GX))
    after = lax.ppermute(first, GX, back(GX))
    applied, yfirst, ylast, weights, wy = inside(
        krylov_block, flux_along, flux_across, collision, wall_mask, wall_type, field_rates,
        wall_table,
    )
    ybefore = lax.ppermute(ylast, GY, onward(GY))
    yafter = lax.ppermute(yfirst, GY, back(GY))
    gp, p_hi, p_lo = basis(prior_basis)
    sizes = [lax.axis_size(stage) for stage in STAGES]
    applied, lines = with_halo(
        applied, p_hi, p_lo, before, after, ybefore, yafter, weights, wy, gp, sizes[0]
    )
    lines = middle(sent_to_all(lines, STAGES[0]), sizes[1])
    lines = sent_to_all(lines, STAGES[1])
    new_block, projection, triangle = final(lines, applied, p_hi, p_lo, cells)
    return new_block, projection.T, triangle


def solution(mesh):
    torus = Mesh(mesh.devices.reshape(8, 4, 4, 2), ("gx_z", "gx_x", "gy_y", "gy_c"))
    cells = P(GX, GY)
    stack = P(None, None, GX, GY)
    in_specs = (stack, stack, P(), P(), cells, P(), P(), cells, cells)
    out_specs = (stack, P(), P())
    return jax.shard_map(
        on_device, mesh=torus, in_specs=in_specs, out_specs=out_specs, check_vma=False
    )
```
